32 devices in a mesh: feat: 4 (over y, x), label: 8 (over z, core).
Axes of the slice: x: 2, y: 2, z: 4, core: 2. Of those that a mesh axis runs over, the one named last changes fastest.
Arguments:
- documents: bfloat16 [160, 1024], P(None, 'label'), may hold values from -6 to 6
- expand_weight: bfloat16 [1024, 32768], P('label', 'feat'), may hold values from -0.1875 to 0.1875
- sparse_weight: bfloat16 [768, 16, 128, 128], P(('feat', 'label')), may hold values from -0.125 to 0.125
- feature_lists: int32 [768, 16], replicated, may hold values from 0 to 255, as said below
- positives: int32 [160, 8], replicated, may hold values from 0 to 98303
Outputs:
- grad_expand: bfloat16 [1024, 32768], P('label', 'feat')
- grad_sparse: bfloat16 [768, 16, 128, 128], P(('feat', 'label'))
The draws below stay inside these ranges and needn't reach their ends.
Inputs may be any that keep to these rules, and one draw needn't show every extreme that they name: `feature_lists`: within each aligned group of 24 label blocks (taken in order), the entries name exactly 24 distinct feature blocks from each range of 64 consecutive blocks, each named exactly 4 times in the group; the 16 entries of one label block are distinct.
All inputs are finite; a program needn't handle non-finite values.
Results may differ from the reference program's by a relative error of at most 0.014.
Values may be sent and summed in bfloat16 or wider, within the bound.
No kernel may reach another device: no remote copies, remote signals or barrier semaphores. Data moves between devices by JAX's collectives and lax.ppermute only.
A program may use at most 192 MiB of HBM per device.

```python
import jax
import jax.numpy as jnp
from jax import lax

D = 1024
BLK = 128
FBLOCKS = 256
SLOTS = 16
LBLK_DEV = 24
CAP = 24
POS = 8
DOCS = 160
H = 32768
LBLKS = 768
LABELS = 98304
N_FEAT = 4


def draw_feature_lists(key, part):
    groups = LBLKS // LBLK_DEV
    per_owner = FBLOCKS // N_FEAT
    pool_size = N_FEAT * CAP
    repeats = LBLK_DEV * SLOTS // pool_size

    def one_group(group_key):
        owner_keys = jax.random.split(jax.random.fold_in(group_key, 11), N_FEAT)
        chosen = jax.vmap(lambda owner_key: jax.random.permutation(owner_key, per_owner)[:CAP])(owner_keys)
        offsets = (jnp.arange(N_FEAT, dtype=jnp.int32) * per_owner)[:, None]
        pool = (chosen.astype(jnp.int32) + offsets).reshape(-1)
        order_keys = jax.random.split(jax.random.fold_in(group_key, 23), repeats)
        orders = jax.vmap(lambda order_key: jax.random.permutation(order_key, pool))(order_keys)
        return orders.reshape(LBLK_DEV, SLOTS).astype(jnp.int32)
    group_keys = jax.random.split(jax.random.fold_in(key, 5), groups)
    return jax.vmap(one_group)(group_keys).reshape(LBLKS, SLOTS).astype(jnp.int32)


def plant(result, key, low, largest):
    dims = result.shape
    index_at = [jax.random.randint(jax.random.fold_in(key, axis), (), 0, dims[axis]) for axis in range(len(dims))]
    result = result.at[tuple(index_at)].set(low)
    longest = dims.index(max(dims))
    index_at[longest] = (index_at[longest] + 1) % dims[longest]
    return result.at[tuple(index_at)].set(largest)


def block_scale(key, extent, cuts, smallest, top_value):
    def one(position, parts):
        draws = jax.random.uniform(jax.random.fold_in(jax.random.fold_in(key, 6), position), (parts,), jnp.float32, smallest / len(cuts), top_value / len(cuts))
        return jnp.repeat(jnp.exp(draws), extent[position] // parts).reshape((-1,) + (1,) * (len(extent) - position - 1))

    factor_of = one(*cuts[0])
    for cut in cuts[1:]:
        factor_of = factor_of * one(*cut)
    return factor_of


def gaussian(rng, shape, width, reach, cuts=(), held_as=jnp.bfloat16):
    gain = block_scale(rng, shape, cuts, -0.22, 0.18) if cuts else 1.0
    entries = jax.random.normal(rng, shape, jnp.float32) * width * gain
    return jnp.minimum(jnp.maximum(entries, -reach), reach).astype(held_as)


def setup_inputs(seed: int = 0) -> dict:
    key_of = jax.random.split(jax.random.key(seed), 6)
    return {
        "documents": gaussian(key_of[0], (DOCS, D), 1.0, 6.0, ((1, 8),)),
        "expand_weight": gaussian(key_of[1], (D, H), D ** -0.5, 0.1875, ((0, 8), (1, 4))),
        "sparse_weight": gaussian(key_of[2], (LBLKS, SLOTS, BLK, BLK), (SLOTS * BLK) ** -0.5, 0.125, ((0, 32),)),
        "feature_lists": draw_feature_lists(jax.random.fold_in(key_of[5], 71), 0),
        "positives": plant(jax.random.randint(key_of[4], (DOCS, POS), 0, LABELS), jax.random.fold_in(key_of[4], 1), 0, LABELS - 1).astype(jnp.int32),
    }


def reference(documents, expand_weight, sparse_weight, feature_lists, positives):
    expanded = jnp.dot(documents, expand_weight, preferred_element_type=jnp.float32)
    hidden = jnp.maximum(expanded, 0.0).astype(jnp.bfloat16)
    hidden_blocks = hidden.reshape(DOCS, FBLOCKS, BLK).transpose(1, 0, 2)
    groups = LBLKS // LBLK_DEV

    def group_step(carry, group):
        lists = lax.dynamic_slice_in_dim(feature_lists, group * LBLK_DEV, LBLK_DEV, 0)
        weights = lax.dynamic_slice_in_dim(sparse_weight, group * LBLK_DEV, LBLK_DEV, 0)
        picked = jnp.take(hidden_blocks, lists, axis=0)
        logits = jnp.einsum("lsdc,lsce->dle", picked.astype(jnp.float32), weights.astype(jnp.float32))
        label_ids = ((group * LBLK_DEV + jnp.arange(LBLK_DEV, dtype=jnp.int32))[:, None] * BLK
                     + jnp.arange(BLK, dtype=jnp.int32)[None, :]).astype(jnp.int32)
        targets = jnp.any(positives[:, :, None, None] == label_ids[None, None, :, :], axis=1).astype(jnp.float32)
        residual = (jax.nn.sigmoid(logits) - targets).astype(jnp.bfloat16)
        grad_block = jnp.einsum("lsdc,dle->lsce", picked.astype(jnp.float32), residual.astype(jnp.float32)).astype(jnp.bfloat16)
        back = jnp.einsum("dle,lsce->lsdc", residual.astype(jnp.float32), weights.astype(jnp.float32))
        partial_value = jax.ops.segment_sum(back.reshape(LBLK_DEV * SLOTS, DOCS, BLK), lists.reshape(-1), num_segments=FBLOCKS)
        partial_value = partial_value.astype(jnp.bfloat16)
        return carry + partial_value.astype(jnp.float32), grad_block

    start = jnp.zeros((FBLOCKS, DOCS, BLK), jnp.float32)
    block_grad, grad_blocks = lax.scan(group_step, start, jnp.arange(groups, dtype=jnp.int32))
    grad_sparse = grad_blocks.reshape(LBLKS, SLOTS, BLK, BLK)
    grad_hidden = jnp.where(hidden_blocks > 0, block_grad, 0.0).astype(jnp.bfloat16)
    grad_expand = jnp.einsum("dk,bdc->kbc", documents.astype(jnp.float32), grad_hidden.astype(jnp.float32))
    grad_expand = grad_expand.reshape(D, FBLOCKS * BLK).astype(jnp.bfloat16)
    return grad_expand, grad_sparse
```

```python
import jax
import jax.numpy as jnp
from jax import lax
from jax.experimental import pallas as pl
from jax.experimental.pallas import tpu as pltpu
from jax.sharding import PartitionSpec as P

BLK = 128
CORES = 2
CHUNKS = 2
UNROLL = 4

BF16 = jnp.bfloat16
F32 = jnp.float32
VMEM = pl.BlockSpec(memory_space=pltpu.VMEM)
SMEM = pl.BlockSpec(memory_space=pltpu.SMEM)
ANY = pl.BlockSpec(memory_space=pl.ANY)


def ring_shift(x, offset):
    count = lax.axis_size("label")
    ring = count // CORES
    pairs = [
        (r * CORES + c, ((r + offset) % ring) * CORES + c)
        for r in range(ring)
        for c in range(CORES)
    ]
    return lax.ppermute(x, "label", pairs)


def swap_cores(x):
    count = lax.axis_size("label")
    return lax.ppermute(x, "label", [(i, i ^ 1) for i in range(count)])


def feat_exchange(x, flip):
    return lax.ppermute(x, "feat", [(i, i ^ flip) for i in range(lax.axis_size("feat"))])


def ring_gather(own):
    ring = lax.axis_size("label") // CORES
    far = ring // 2
    half = own.shape[0] // 2
    pieces = [None] * ring
    pieces[0] = own
    up = down = own
    for step in range(1, far):
        up = ring_shift(up, 1)
        down = ring_shift(down, -1)
        pieces[(-step) % ring] = up
        pieces[step] = down
    first = ring_shift(up[:half], 1)
    second = ring_shift(down[half:], -1)
    pieces[far] = jnp.concatenate([first, second], axis=0)
    return pieces


def ring_reduce(pieces):
    ring = len(pieces)
    far = ring // 2
    half = pieces[0].shape[0] // 2
    up = ring_shift(pieces[far][:half], 1)
    down = ring_shift(pieces[far][half:], -1)
    for step in range(far - 1, 0, -1):
        ahead = pieces[step].astype(F32)
        behind = pieces[(-step) % ring].astype(F32)
        if step == far - 1:
            ahead = jnp.concatenate([ahead[:half] + up.astype(F32), ahead[half:]], axis=0)
            behind = jnp.concatenate([behind[:half], behind[half:] + down.astype(F32)], axis=0)
        else:
            ahead = ahead + up.astype(F32)
            behind = behind + down.astype(F32)
        up = ring_shift(ahead.astype(BF16), 1)
        down = ring_shift(behind.astype(BF16), -1)
    return [pieces[0].astype(F32), up.astype(F32), down.astype(F32)]


def select_blocks(pools, index, cap):
    size, docs, blk = pools[0].shape
    outs = index.shape[0] // cap

    def kernel(index_ref, *refs):
        ins = refs[: len(pools)]
        out_refs = refs[len(pools) : len(pools) + outs]
        pool, sem = refs[len(pools) + outs :]
        copies = [
            pltpu.make_async_copy(ref, pool.at[pl.ds(i * size, size)], sem.at[i])
            for i, ref in enumerate(ins)
        ]
        for copy in copies:
            copy.start()
        for copy in copies:
            copy.wait()
        for m in range(outs):

            def step(k, carry):
                out_refs[m][k] = pool[index_ref[m * cap + k]]
                return carry

            lax.fori_loop(0, cap, step, 0, unroll=UNROLL)

    return pl.pallas_call(
        kernel,
        out_shape=[jax.ShapeDtypeStruct((cap, docs, blk), BF16)] * outs,
        in_specs=[SMEM] + [ANY] * len(pools),
        out_specs=[VMEM] * outs,
        scratch_shapes=[
            pltpu.VMEM((len(pools) * size, docs, blk), BF16),
            pltpu.SemaphoreType.DMA((len(pools),)),
        ],
        name="select_blocks",
    )(index, *pools)


def add_blocks(parts, index, blocks, outs):
    cap, docs, blk = parts[0].shape
    size = blocks // outs

    def kernel(index_ref, *refs):
        ins = refs[: len(parts)]
        out_refs = refs[len(parts) : len(parts) + outs]
        total = refs[-1]
        total[...] = jnp.zeros_like(total)
        for m, ref in enumerate(ins):

            def step(k, carry):
                total[index_ref[m * cap + k]] += ref[k].astype(F32)
                return carry

            lax.fori_loop(0, cap, step, 0, unroll=UNROLL)
        for i, ref in enumerate(out_refs):
            ref[...] = total[pl.ds(i * size, size)].astype(BF16)

    return pl.pallas_call(
        kernel,
        out_shape=[jax.ShapeDtypeStruct((size, docs, blk), BF16)] * outs,
        in_specs=[SMEM] + [VMEM] * len(parts),
        out_specs=[VMEM] * outs,
        scratch_shapes=[pltpu.VMEM((blocks, docs, blk), F32)],
        name="add_blocks",
    )(index, *parts)


def residual_and_back(parts, weight, slot_position, order, positives, first_label):
    count = len(parts)
    cap, docs, blk = parts[0].shape
    label_blocks, slots = weight.shape[:2]
    uses = label_blocks * slots // (count * cap)
    pos_count = positives.shape[1]

    def kernel(position_ref, order_ref, first_ref, positives_ref, weight_hbm, *refs):
        ins = refs[:count]
        residual_ref = refs[count]
        outs = refs[count + 1 : 2 * count + 1]
        pool, weight_ref, pool_sem, weight_sem = refs[2 * count + 1 :]
        copies = [
            pltpu.make_async_copy(ins[q], pool.at[pl.ds(q * cap, cap)], pool_sem.at[q])
            for q in range(count)
        ]
        loads = [
            pltpu.make_async_copy(
                weight_hbm.at[g], weight_ref.at[pl.ds(g * slots, slots)], weight_sem.at[g]
            )
            for g in range(label_blocks)
        ]
        for copy in copies + loads:
            copy.start()
        for copy in copies:
            copy.wait()

        def forward(g, carry):
            pltpu.make_async_copy(
                weight_hbm.at[g], weight_ref.at[pl.ds(g * slots, slots)], weight_sem.at[g]
            ).wait()
            lhs = jnp.concatenate(
                [pool[position_ref[g * slots + s]] for s in range(slots)], axis=1
            )
            rhs = weight_ref[pl.ds(g * slots, slots)].reshape(slots * blk, blk)
            logits = jnp.dot(lhs, rhs, preferred_element_type=F32)
            ids = first_ref[0] + g * blk + lax.broadcasted_iota(jnp.int32, (docs, blk), 1)
            hit = positives_ref[:, 0:1] == ids
            for p in range(1, pos_count):
                hit = hit | (positives_ref[:, p : p + 1] == ids)
            residual_ref[g] = (jax.nn.sigmoid(logits) - jnp.where(hit, 1.0, 0.0)).astype(BF16)
            return carry

        lax.fori_loop(0, label_blocks, forward, 0, unroll=UNROLL)
        for q in range(count):

            def backward(k, carry):
                where = [order_ref[(q * cap + k) * uses + u] for u in range(uses)]
                lhs = jnp.concatenate([residual_ref[w // slots] for w in where], axis=1)
                rhs = jnp.concatenate([weight_ref[w] for w in where], axis=1)
                outs[q][k] = lax.dot_general(
                    lhs, rhs, (((1,), (1,)), ((), ())), preferred_element_type=F32
                ).astype(BF16)
                return carry

            lax.fori_loop(0, cap, backward, 0, unroll=2 * UNROLL)

    out = pl.pallas_call(
        kernel,
        out_shape=[jax.ShapeDtypeStruct((label_blocks, docs, blk), BF16)]
        + [jax.ShapeDtypeStruct((cap, docs, blk), BF16)] * count,
        in_specs=[SMEM] * 3 + [VMEM] + [ANY] * (count + 1),
        out_specs=[VMEM] * (count + 1),
        scratch_shapes=[
            pltpu.VMEM((count * cap, docs, blk), BF16),
            pltpu.VMEM((label_blocks * slots, blk, blk), BF16),
            pltpu.SemaphoreType.DMA((count,)),
            pltpu.SemaphoreType.DMA((label_blocks,)),
        ],
        name="residual_and_back",
    )(slot_position, order, first_label, positives, weight, *parts)
    return out[0], list(out[1:])


def block_weight_grad(chunks, residuals, order, label_blocks, slots):
    pieces = len(chunks)
    count = len(chunks[0])
    cap, _, blk = chunks[0][0].shape
    docs = [chunk[0].shape[1] for chunk in chunks]
    uses = label_blocks * slots // (count * cap)

    def kernel(order_ref, *refs):
        residual_refs = refs[:pieces]
        ins = refs[pieces : pieces + pieces * count]
        out_ref = refs[pieces + pieces * count]
        pools = refs[pieces + pieces * count + 1 :][:pieces]
        buffer, sem, out_sem = refs[-3:]
        copies = [
            pltpu.make_async_copy(
                ins[i * count + q], pools[i].at[pl.ds(q * cap, cap)], sem.at[i * count + q]
            )
            for i in range(pieces)
            for q in range(count)
        ]
        for copy in copies:
            copy.start()
        for copy in copies:
            copy.wait()

        def step(k, carry):
            where = [order_ref[k * uses + u] for u in range(uses)]
            rhs = jnp.concatenate(
                [
                    jnp.concatenate([ref[w // slots] for w in where], axis=1)
                    for ref in residual_refs
                ],
                axis=0,
            )
            lhs = jnp.concatenate([pool[k] for pool in pools], axis=0)
            out = lax.dot_general(
                lhs, rhs, (((0,), (0,)), ((), ())), preferred_element_type=F32
            ).astype(BF16)
            for u in range(uses):
                buffer[k * uses + u] = out[:, u * blk : (u + 1) * blk]
                pltpu.make_async_copy(
                    buffer.at[k * uses + u], out_ref.at[where[u]], out_sem
                ).start()
            return carry

        lax.fori_loop(0, count * cap, step, 0, unroll=UNROLL)
        pltpu.make_async_copy(buffer, out_ref, out_sem).wait()

    out = pl.pallas_call(
        kernel,
        out_shape=jax.ShapeDtypeStruct((label_blocks * slots, blk, blk), BF16),
        in_specs=[SMEM] + [VMEM] * pieces + [ANY] * (pieces * count),
        out_specs=ANY,
        scratch_shapes=[pltpu.VMEM((count * cap, d, blk), BF16) for d in docs]
        + [
            pltpu.VMEM((label_blocks * slots, blk, blk), BF16),
            pltpu.SemaphoreType.DMA((pieces * count,)),
            pltpu.SemaphoreType.DMA(()),
        ],
        name="block_weight_grad",
    )(order, *residuals, *[part for chunk in chunks for part in chunk])
    return out.reshape(label_blocks, slots, blk, blk)


def expand_weight_grad(documents, groups, columns, width):
    pieces = len(groups)
    chunks = len(groups[0])
    size, _, blk = groups[0][0].shape
    docs_all, rows = documents.shape

    def kernel(columns_ref, documents_ref, *refs):
        out_ref = refs[-1]
        lhs = documents_ref[...]
        for i in range(pieces):
            ins = refs[i * chunks : (i + 1) * chunks]
            rhs = jnp.concatenate(
                [jnp.concatenate([ref[j] for ref in ins], axis=0) for j in range(size)], axis=1
            )
            out = lax.dot_general(
                lhs, rhs, (((0,), (0,)), ((), ())), preferred_element_type=F32
            )
            start = pl.multiple_of(columns_ref[i], blk)
            out_ref[:, pl.ds(start, size * blk)] = out.astype(BF16)

    return pl.pallas_call(
        kernel,
        out_shape=jax.ShapeDtypeStruct((rows, width), BF16),
        in_specs=[SMEM, VMEM] + [VMEM] * (pieces * chunks),
        out_specs=VMEM,
        name="expand_weight_grad",
    )(columns, documents, *[part for group in groups for part in group])


def list_tables(feature_lists, feat_index, label_index, label_count, own_count, label_blocks, cap):
    feat_count = lax.axis_size("feat")
    slots = feature_lists.shape[1]
    entries = label_blocks * slots
    ring = label_count // CORES
    own_blocks = own_count // label_count
    flips = jnp.arange(feat_count, dtype=jnp.int32)
    by_device = feature_lists.reshape(feat_count, label_count, entries)
    column = lax.dynamic_index_in_dim(by_device, label_index, 1, keepdims=False)
    mine = lax.dynamic_index_in_dim(column, feat_index, 0, keepdims=False)

    local = jnp.arange(own_count, dtype=jnp.int32)
    wanted = jnp.any(
        column[:, :, None] == (feat_index * own_count + local)[None, None, :], axis=1
    )
    rank = jnp.sum(wanted[:, None, :] & (local[None, :] < local[:, None])[None], axis=2)
    chosen = wanted[:, None, :] & (rank[:, None, :] == jnp.arange(cap)[None, :, None])
    ring_index, core = label_index // CORES, label_index % CORES
    owner_ring = local // (CORES * own_blocks)
    owner_core = local // own_blocks % CORES
    place = (
        jnp.where(owner_core == core, 0, ring) + (owner_ring - ring_index) % ring
    ) * own_blocks + local % own_blocks
    send = jnp.sum(jnp.where(chosen, place[None, None, :], 0), axis=2).astype(jnp.int32)
    send = jnp.stack(
        [lax.dynamic_index_in_dim(send, feat_index ^ m, 0, keepdims=False) for m in range(feat_count)]
    ).reshape(-1)

    block = jnp.arange(feat_count * own_count, dtype=jnp.int32)
    present = jnp.any(mine[:, None] == block[None, :], axis=0)
    before = jnp.sum(
        present[None, :]
        & (block[None, :] // own_count == block[:, None] // own_count)
        & (block[None, :] < block[:, None]),
        axis=1,
    )
    table = ((block // own_count) ^ feat_index) * cap + before
    position = jnp.sum(
        jnp.where(mine[:, None] == block[None, :], table[None, :], 0), axis=1
    ).astype(jnp.int32)
    entry = jnp.arange(entries, dtype=jnp.int32)
    earlier = jnp.sum((mine[None, :] == mine[:, None]) & (entry[None, :] < entry[:, None]), axis=1)
    uses = entries // (feat_count * cap)
    key = position * uses + earlier
    order = jnp.sum(jnp.where(key[None, :] == entry[:, None], entry[None, :], 0), axis=1)
    return send, position, order.astype(jnp.int32)


def on_device(documents, expand_weight, sparse_weight, feature_lists, positives):
    feat_count = lax.axis_size("feat")
    label_count = lax.axis_size("label")
    feat_index = lax.axis_index("feat")
    label_index = lax.axis_index("label")
    group = feat_index * label_count + label_index
    ring = label_count // CORES
    far = ring // 2
    ring_index, core = label_index // CORES, label_index % CORES
    docs = documents.shape[0]
    rows, width = expand_weight.shape
    own_count = width // BLK
    own_blocks = own_count // label_count
    label_blocks, slots = sparse_weight.shape[:2]
    cap = CAP
    chunk = docs // CHUNKS
    cuts = [slice(i * chunk, (i + 1) * chunk) for i in range(CHUNKS)]

    ring_width = width // ring

    def columns_of(offset):
        start = (ring_index + offset) % ring * ring_width
        return lax.dynamic_slice_in_dim(expand_weight, start, ring_width, 1)

    far_columns = columns_of(far)
    half = rows // 2
    up, down = far_columns[:half], far_columns[half:]
    up = ring_shift(up, 1)
    down = ring_shift(down, -1)
    arrived = {}
    for offset in range(1, ring):
        if offset != far:
            arrived[offset] = ring_shift(columns_of(offset), offset)
    for _ in range(far - 1):
        up = ring_shift(up, 1)
        down = ring_shift(down, -1)
    others = {offset: ring_shift(documents, offset) for offset in range(1, ring)}

    def product(left, right):
        right = right.reshape(right.shape[0], ring_width // BLK, BLK)
        return jnp.einsum("dk,kbc->bdc", left, right, preferred_element_type=F32)

    expanded = product(documents, columns_of(0))
    for offset in range(1, ring):
        if offset != far:
            expanded = expanded + product(others[offset], arrived[offset])
    expanded = expanded + product(others[far], jnp.concatenate([up, down], axis=0))
    kept = lax.dynamic_slice_in_dim(expanded, core * own_blocks, own_blocks, 0)
    given = lax.dynamic_slice_in_dim(expanded, (1 - core) * own_blocks, own_blocks, 0)
    hidden = jnp.maximum(kept + swap_cores(given), 0.0).astype(BF16)

    send, position, order = list_tables(
        feature_lists, feat_index, label_index, label_count, own_count, label_blocks, cap
    )
    first_label = (group * label_blocks * BLK).reshape(1)

    picked, residuals, gradients = [], [], []
    for cut in cuts:
        pool = jnp.concatenate(ring_gather(hidden[:, cut]), axis=0)
        outgoing = select_blocks([pool, swap_cores(pool)], send, cap)
        parts = [outgoing[0]] + [feat_exchange(outgoing[m], m) for m in range(1, feat_count)]
        residual, back = residual_and_back(
            parts, sparse_weight, position, order, positives[cut], first_label
        )
        picked.append(parts)
        residuals.append(residual)
        returned = [back[0]] + [feat_exchange(back[m], m) for m in range(1, feat_count)]
        kept, given = add_blocks(returned, send, own_count, CORES)
        both = (kept.astype(F32) + swap_cores(given).astype(F32)).astype(BF16)
        terms = ring_reduce([both[k * own_blocks : (k + 1) * own_blocks] for k in range(ring)])
        gradient = jnp.where(hidden[:, cut] > 0, sum(terms), 0.0).astype(BF16)
        gathered = jnp.concatenate(ring_gather(gradient), axis=0)
        gradients.append((gathered, swap_cores(gathered)))

    grad_sparse = block_weight_grad(picked, residuals, order, label_blocks, slots)

    groups, starts = [], []
    for side in range(CORES):
        for k in range(ring):
            groups.append(
                [g[side][k * own_blocks : (k + 1) * own_blocks] for g in gradients]
            )
            starts.append(
                (((ring_index + k) % ring) * CORES + (core ^ side)) * own_blocks * BLK
            )
    grad_expand = expand_weight_grad(documents, groups, jnp.stack(starts), width)
    return (grad_expand, grad_sparse)


CAP = 24


def solution(mesh):
    return jax.shard_map(
        on_device,
        mesh=mesh,
        in_specs=(
            P(None, "label"),
            P("label", "feat"),
            P(("feat", "label"), None, None, None),
            P(),
            P(),
        ),
        out_specs=(P("label", "feat"), P(("feat", "label"), None, None, None)),
        check_vma=False,
    )
```

```python
import jax
import jax.numpy as jnp
from jax import lax
from jax.experimental import pallas as pl
from jax.experimental.pallas import tpu as pltpu
from jax.sharding import PartitionSpec as P


BLK = 128
CAP = 24
CORES = 2
CHUNKS = 2
UNROLL = 4

BF16 = jnp.bfloat16
F32 = jnp.float32
VMEM = pl.BlockSpec(memory_space=pltpu.VMEM)
SMEM = pl.BlockSpec(memory_space=pltpu.SMEM)
ANY = pl.BlockSpec(memory_space=pl.ANY)


def ring_exchange(x, flip):
    count = lax.axis_size("label")
    return lax.ppermute(x, "label", [(i, i ^ (flip * CORES)) for i in range(count)])


def swap_cores(x):
    count = lax.axis_size("label")
    return lax.ppermute(x, "label", [(i, i ^ 1) for i in range(count)])


def feat_exchange(x, flip):
    return lax.ppermute(x, "feat", [(i, i ^ flip) for i in range(lax.axis_size("feat"))])


def ring_gather(own):
    ring = lax.axis_size("label") // CORES
    return [own] + [ring_exchange(own, k) for k in range(1, ring)]


def cut_columns(weight, starts, width):
    count = starts.shape[0]

    def kernel(starts_ref, weight_hbm, *refs):
        outs, sem = refs[:count], refs[count]
        copies = [
            pltpu.make_async_copy(
                weight_hbm.at[:, pl.ds(pl.multiple_of(starts_ref[k], BLK), width)], out, sem.at[k]
            )
            for k, out in enumerate(outs)
        ]
        for copy in copies:
            copy.start()
        for copy in copies:
            copy.wait()

    return pl.pallas_call(
        kernel,
        out_shape=[jax.ShapeDtypeStruct((weight.shape[0], width), weight.dtype)] * count,
        in_specs=[SMEM, ANY],
        out_specs=[ANY] * count,
        scratch_shapes=[pltpu.SemaphoreType.DMA((count,))],
        name="cut_columns",
    )(starts, weight)


def select_blocks(pools, index, cap):
    size, docs, blk = pools[0].shape
    outs = index.shape[0] // cap

    def kernel(index_ref, *refs):
        ins = refs[: len(pools)]
        out_refs = refs[len(pools) :]
        for m in range(outs):

            def step(k, carry):
                place = index_ref[m * cap + k]
                block = ins[0][place % size]
                for i in range(1, len(ins)):
                    block = jnp.where(place >= i * size, ins[i][place % size], block)
                out_refs[m][k] = block
                return carry

            lax.fori_loop(0, cap, step, 0, unroll=UNROLL)

    return pl.pallas_call(
        kernel,
        out_shape=[jax.ShapeDtypeStruct((cap, docs, blk), BF16)] * outs,
        in_specs=[SMEM] + [VMEM] * len(pools),
        out_specs=[VMEM] * outs,
        name="select_blocks",
    )(index, *pools)


def add_blocks(parts, index, blocks, outs):
    cap, docs, blk = parts[0].shape
    size = blocks // outs

    def kernel(index_ref, *refs):
        ins = refs[: len(parts)]
        out_refs = refs[len(parts) : len(parts) + outs]
        total = refs[-1]
        total[...] = jnp.zeros_like(total)
        for m, ref in enumerate(ins):

            def step(k, carry):
                total[index_ref[m * cap + k]] += ref[k].astype(F32)
                return carry

            lax.fori_loop(0, cap, step, 0, unroll=UNROLL)
        for i, ref in enumerate(out_refs):
            ref[...] = total[pl.ds(i * size, size)].astype(BF16)

    return pl.pallas_call(
        kernel,
        out_shape=[jax.ShapeDtypeStruct((size, docs, blk), BF16)] * outs,
        in_specs=[SMEM] + [VMEM] * len(parts),
        out_specs=[VMEM] * outs,
        scratch_shapes=[pltpu.VMEM((blocks, docs, blk), F32)],
        name="add_blocks",
    )(index, *parts)


def residual_and_back(parts, weight, slot_position, order, positives, first_label):
    count = len(parts)
    cap, docs, blk = parts[0].shape
    label_blocks, slots = weight.shape[:2]
    uses = label_blocks * slots // (count * cap)
    pos_count = positives.shape[1]

    def kernel(position_ref, order_ref, first_ref, positives_ref, weight_hbm, *refs):
        ins = refs[:count]
        residual_ref = refs[count]
        outs = refs[count + 1 : 2 * count + 1]
        pool, weight_ref, pool_sem, weight_sem = refs[2 * count + 1 :]
        copies = [
            pltpu.make_async_copy(ins[q], pool.at[pl.ds(q * cap, cap)], pool_sem.at[q])
            for q in range(count)
        ]
        loads = [
            pltpu.make_async_copy(
                weight_hbm.at[g], weight_ref.at[pl.ds(g * slots, slots)], weight_sem.at[g]
            )
            for g in range(label_blocks)
        ]
        for copy in copies + loads:
            copy.start()
        for copy in copies:
            copy.wait()

        def forward(g, carry):
            pltpu.make_async_copy(
                weight_hbm.at[g], weight_ref.at[pl.ds(g * slots, slots)], weight_sem.at[g]
            ).wait()
            lhs = jnp.concatenate(
                [pool[position_ref[g * slots + s]] for s in range(slots)], axis=1
            )
            rhs = weight_ref[pl.ds(g * slots, slots)].reshape(slots * blk, blk)
            logits = jnp.dot(lhs, rhs, preferred_element_type=F32)
            ids = first_ref[0] + g * blk + lax.broadcasted_iota(jnp.int32, (docs, blk), 1)
            hit = positives_ref[:, 0:1] == ids
            for p in range(1, pos_count):
                hit = hit | (positives_ref[:, p : p + 1] == ids)
            residual_ref[g] = (jax.nn.sigmoid(logits) - jnp.where(hit, 1.0, 0.0)).astype(BF16)
            return carry

        lax.fori_loop(0, label_blocks, forward, 0, unroll=UNROLL)
        for q in range(count):

            def backward(k, carry):
                where = [order_ref[(q * cap + k) * uses + u] for u in range(uses)]
                lhs = jnp.concatenate([residual_ref[w // slots] for w in where], axis=1)
                rhs = jnp.concatenate([weight_ref[w] for w in where], axis=1)
                outs[q][k] = lax.dot_general(
                    lhs, rhs, (((1,), (1,)), ((), ())), preferred_element_type=F32
                ).astype(BF16)
                return carry

            lax.fori_loop(0, cap, backward, 0, unroll=2 * UNROLL)

    out = pl.pallas_call(
        kernel,
        out_shape=[jax.ShapeDtypeStruct((label_blocks, docs, blk), BF16)]
        + [jax.ShapeDtypeStruct((cap, docs, blk), BF16)] * count,
        in_specs=[SMEM] * 3 + [VMEM, ANY] + [VMEM] * count,
        out_specs=[VMEM] * (count + 1),
        scratch_shapes=[
            pltpu.VMEM((count * cap, docs, blk), BF16),
            pltpu.VMEM((label_blocks * slots, blk, blk), BF16),
            pltpu.SemaphoreType.DMA((count,)),
            pltpu.SemaphoreType.DMA((label_blocks,)),
        ],
        name="residual_and_back",
    )(slot_position, order, first_label, positives, weight, *parts)
    return out[0], list(out[1:])


def block_weight_grad(chunks, residuals, order, label_blocks, slots):
    pieces = len(chunks)
    count = len(chunks[0])
    cap, _, blk = chunks[0][0].shape
    uses = label_blocks * slots // (count * cap)

    def kernel(order_ref, *refs):
        residual_refs = refs[:pieces]
        ins = refs[pieces : pieces + pieces * count]
        out_ref = refs[pieces + pieces * count]
        buffer, out_sem = refs[pieces + pieces * count + 1 :]
        for q in range(count):
            pools = [ins[i * count + q] for i in range(pieces)]

            def step(j, carry):
                k = q * cap + j
                where = [order_ref[k * uses + u] for u in range(uses)]
                rhs = jnp.concatenate(
                    [
                        jnp.concatenate([ref[w // slots] for w in where], axis=1)
                        for ref in residual_refs
                    ],
                    axis=0,
                )
                lhs = jnp.concatenate([pool[j] for pool in pools], axis=0)
                out = lax.dot_general(
                    lhs, rhs, (((0,), (0,)), ((), ())), preferred_element_type=F32
                ).astype(BF16)
                for u in range(uses):
                    buffer[k * uses + u] = out[:, u * blk : (u + 1) * blk]
                    pltpu.make_async_copy(
                        buffer.at[k * uses + u], out_ref.at[where[u]], out_sem
                    ).start()
                return carry

            lax.fori_loop(0, cap, step, 0, unroll=UNROLL)
        pltpu.make_async_copy(buffer, out_ref, out_sem).wait()

    out = pl.pallas_call(
        kernel,
        out_shape=jax.ShapeDtypeStruct((label_blocks * slots, blk, blk), BF16),
        in_specs=[SMEM] + [VMEM] * (pieces + pieces * count),
        out_specs=ANY,
        scratch_shapes=[
            pltpu.VMEM((label_blocks * slots, blk, blk), BF16),
            pltpu.SemaphoreType.DMA(()),
        ],
        name="block_weight_grad",
    )(order, *residuals, *[part for chunk in chunks for part in chunk])
    return out.reshape(label_blocks, slots, blk, blk)


def expand_weight_grad(documents, groups, columns, width):
    pieces = len(groups)
    chunks = len(groups[0])
    size, _, blk = groups[0][0].shape
    _, rows = documents.shape

    def kernel(columns_ref, documents_ref, *refs):
        out_ref = refs[-1]
        lhs = documents_ref[...]
        for i in range(pieces):
            ins = refs[i * chunks : (i + 1) * chunks]
            rhs = jnp.concatenate(
                [jnp.concatenate([ref[j] for ref in ins], axis=0) for j in range(size)], axis=1
            )
            out = lax.dot_general(
                lhs, rhs, (((0,), (0,)), ((), ())), preferred_element_type=F32
            )
            start = pl.multiple_of(columns_ref[i], blk)
            out_ref[:, pl.ds(start, size * blk)] = out.astype(BF16)

    return pl.pallas_call(
        kernel,
        out_shape=jax.ShapeDtypeStruct((rows, width), BF16),
        in_specs=[SMEM, VMEM] + [VMEM] * (pieces * chunks),
        out_specs=VMEM,
        name="expand_weight_grad",
    )(columns, documents, *[part for group in groups for part in group])


def list_tables(feature_lists, feat_index, label_index, label_count, own_count, label_blocks, cap):
    feat_count = lax.axis_size("feat")
    slots = feature_lists.shape[1]
    entries = label_blocks * slots
    ring = label_count // CORES
    own_blocks = own_count // label_count
    flips = jnp.arange(feat_count, dtype=jnp.int32)
    by_device = feature_lists.reshape(feat_count, label_count, entries)
    column = lax.dynamic_index_in_dim(by_device, label_index, 1, keepdims=False)
    mine = lax.dynamic_index_in_dim(column, feat_index, 0, keepdims=False)

    local = jnp.arange(own_count, dtype=jnp.int32)
    wanted = jnp.any(
        column[:, :, None] == (feat_index * own_count + local)[None, None, :], axis=1
    )
    rank = jnp.sum(wanted[:, None, :] & (local[None, :] < local[:, None])[None], axis=2)
    chosen = wanted[:, None, :] & (rank[:, None, :] == jnp.arange(cap)[None, :, None])
    ring_index, core = label_index // CORES, label_index % CORES
    owner_ring = local // (CORES * own_blocks)
    owner_core = local // own_blocks % CORES
    place = (
        jnp.where(owner_core == core, 0, ring) + (owner_ring ^ ring_index)
    ) * own_blocks + local % own_blocks
    send = jnp.sum(jnp.where(chosen, place[None, None, :], 0), axis=2).astype(jnp.int32)
    send = jnp.stack(
        [lax.dynamic_index_in_dim(send, feat_index ^ m, 0, keepdims=False) for m in range(feat_count)]
    ).reshape(-1)

    block = jnp.arange(feat_count * own_count, dtype=jnp.int32)
    present = jnp.any(mine[:, None] == block[None, :], axis=0)
    before = jnp.sum(
        present[None, :]
        & (block[None, :] // own_count == block[:, None] // own_count)
        & (block[None, :] < block[:, None]),
        axis=1,
    )
    table = ((block // own_count) ^ feat_index) * cap + before
    position = jnp.sum(
        jnp.where(mine[:, None] == block[None, :], table[None, :], 0), axis=1
    ).astype(jnp.int32)
    entry = jnp.arange(entries, dtype=jnp.int32)
    earlier = jnp.sum((mine[None, :] == mine[:, None]) & (entry[None, :] < entry[:, None]), axis=1)
    uses = entries // (feat_count * cap)
    key = position * uses + earlier
    order = jnp.sum(jnp.where(key[None, :] == entry[:, None], entry[None, :], 0), axis=1)
    return send, position, order.astype(jnp.int32)


def program(documents, expand_weight, sparse_weight, feature_lists, positives):
    feat_count = lax.axis_size("feat")
    label_count = lax.axis_size("label")
    feat_index = lax.axis_index("feat")
    label_index = lax.axis_index("label")
    group = feat_index * label_count + label_index
    ring = label_count // CORES
    ring_index, core = label_index // CORES, label_index % CORES
    docs = documents.shape[0]
    _, width = expand_weight.shape
    own_count = width // BLK
    own_blocks = own_count // label_count
    label_blocks, slots = sparse_weight.shape[:2]
    cap = CAP
    chunk = docs // CHUNKS
    cuts = [slice(i * chunk, (i + 1) * chunk) for i in range(CHUNKS)]

    ring_width = width // ring
    starts = (jnp.arange(ring, dtype=jnp.int32) ^ ring_index) * ring_width

    def product(left, right):
        right = right.reshape(right.shape[0], ring_width // BLK, BLK)
        return jnp.einsum("dk,kbc->bdc", left, right, preferred_element_type=F32)

    columns = cut_columns(expand_weight, starts, ring_width)
    arrived = [columns[0]] + [None] * (ring - 1)
    for k in range(ring - 1, 0, -1):
        arrived[k] = ring_exchange(columns[k], k)
    documents_late, _ = lax.optimization_barrier((documents, columns[0]))
    expanded = product(documents, columns[0])
    for k in range(1, ring):
        other = ring_exchange(documents_late, k)
        expanded = expanded + product(other, arrived[k])
    kept = lax.dynamic_slice_in_dim(expanded, core * own_blocks, own_blocks, 0)
    given = lax.dynamic_slice_in_dim(expanded, (1 - core) * own_blocks, own_blocks, 0)

    send, position, order = list_tables(
        feature_lists, feat_index, label_index, label_count, own_count, label_blocks, cap
    )
    first_label = (group * label_blocks * BLK).reshape(1)
    known = [positives[cut] for cut in cuts]
    given, send, position, order, known, first_label = lax.optimization_barrier(
        (given, send, position, order, known, first_label)
    )
    hidden = jnp.maximum(kept + swap_cores(given), 0.0).astype(BF16)

    picked, residuals, gradients = [], [], []
    for i, cut in enumerate(cuts):
        pool = jnp.concatenate(ring_gather(hidden[:, cut]), axis=0)
        pools = [pool, swap_cores(pool)]
        outgoing = select_blocks(pools, send, cap)
        parts = [outgoing[0]] + [None] * (feat_count - 1)
        for m in range(feat_count - 1, 0, -1):
            parts[m] = feat_exchange(outgoing[m], m)
        residual, back = residual_and_back(
            parts, sparse_weight, position, order, known[i], first_label
        )
        picked.append(parts)
        residuals.append(residual)
        returned = [back[0]] + [None] * (feat_count - 1)
        for m in range(feat_count - 1, 0, -1):
            returned[m] = feat_exchange(back[m], m)
        kept, given = add_blocks(returned, send, own_count, CORES)
        both = (kept.astype(F32) + swap_cores(given).astype(F32)).astype(BF16)
        pieces = [both[k * own_blocks : (k + 1) * own_blocks] for k in range(ring)]
        total = pieces[0].astype(F32)
        for k in range(ring - 1, 0, -1):
            total = total + ring_exchange(pieces[k], k).astype(F32)
        if gradients:
            total, _ = lax.optimization_barrier((total, gradients[-1][0]))
        gradient = jnp.where(hidden[:, cut] > 0, total, 0.0).astype(BF16)
        gathered = jnp.concatenate(ring_gather(gradient), axis=0)
        gradients.append((gathered, swap_cores(gathered)))

    grad_sparse = block_weight_grad(picked, residuals, order, label_blocks, slots)

    groups, starts = [], []
    for side in range(CORES):
        for k in range(ring):
            groups.append(
                [g[side][k * own_blocks : (k + 1) * own_blocks] for g in gradients]
            )
            starts.append(
                ((ring_index ^ k) * CORES + (core ^ side)) * own_blocks * BLK
            )
    grad_expand = expand_weight_grad(documents, groups, jnp.stack(starts), width)
    return (grad_expand, grad_sparse)


def solution(mesh):
    return jax.shard_map(
        program,
        mesh=mesh,
        in_specs=(
            P(None, "label"),
            P("label", "feat"),
            P(("feat", "label"), None, None, None),
            P(),
            P(),
        ),
        out_specs=(P("label", "feat"), P(("feat", "label"), None, None, None)),
        check_vma=False,
    )
```

```python
import jax
import jax.numpy as jnp
from jax import lax
from jax.experimental import pallas as pl
from jax.experimental.pallas import tpu as pltpu
from jax.sharding import PartitionSpec as P


BLK = 128
CAP = 24
CORES = 2
CHUNKS = 2
UNROLL = 4

BF16 = jnp.bfloat16
F32 = jnp.float32
VMEM = pl.BlockSpec(memory_space=pltpu.VMEM)
SMEM = pl.BlockSpec(memory_space=pltpu.SMEM)
ANY = pl.BlockSpec(memory_space=pl.ANY)


def ring_exchange(x, flip):
    count = lax.axis_size("label")
    return lax.ppermute(x, "label", [(i, i ^ (flip * CORES)) for i in range(count)])


def swap_cores(x):
    count = lax.axis_size("label")
    return lax.ppermute(x, "label", [(i, i ^ 1) for i in range(count)])


def feat_exchange(x, flip):
    return lax.ppermute(x, "feat", [(i, i ^ flip) for i in range(lax.axis_size("feat"))])


def ring_gather(own):
    ring = lax.axis_size("label") // CORES
    return [own] + [ring_exchange(own, k) for k in range(1, ring)]


def cut_columns(weight, starts, width):
    count = starts.shape[0]

    def kernel(starts_ref, weight_ref, *outs):
        for k, out in enumerate(outs):
            out[...] = weight_ref[:, pl.ds(pl.multiple_of(starts_ref[k], BLK), width)]

    return pl.pallas_call(
        kernel,
        out_shape=[jax.ShapeDtypeStruct((weight.shape[0], width), weight.dtype)] * count,
        in_specs=[SMEM, VMEM],
        out_specs=[VMEM] * count,
        name="cut_columns",
    )(starts, weight)


def select_blocks(pools, index, cap):
    size, docs, blk = pools[0].shape
    outs = index.shape[0] // cap

    def kernel(index_ref, *refs):
        ins = refs[: len(pools)]
        out_refs = refs[len(pools) :]
        for m in range(outs):

            def step(k, carry):
                place = index_ref[m * cap + k]
                block = ins[0][place % size]
                for i in range(1, len(ins)):
                    block = jnp.where(place >= i * size, ins[i][place % size], block)
                out_refs[m][k] = block
                return carry

            lax.fori_loop(0, cap, step, 0, unroll=UNROLL)

    return pl.pallas_call(
        kernel,
        out_shape=[jax.ShapeDtypeStruct((cap, docs, blk), BF16)] * outs,
        in_specs=[SMEM] + [VMEM] * len(pools),
        out_specs=[VMEM] * outs,
        name="select_blocks",
    )(index, *pools)


def add_blocks(parts, index, blocks, outs):
    cap, docs, blk = parts[0].shape
    size = blocks // outs

    def kernel(index_ref, *refs):
        ins = refs[: len(parts)]
        out_refs = refs[len(parts) : len(parts) + outs]
        total = refs[-1]
        total[...] = jnp.zeros_like(total)
        for m, ref in enumerate(ins):

            def step(k, carry):
                total[index_ref[m * cap + k]] += ref[k].astype(F32)
                return carry

            lax.fori_loop(0, cap, step, 0, unroll=UNROLL)
        for i, ref in enumerate(out_refs):
            ref[...] = total[pl.ds(i * size, size)].astype(BF16)

    return pl.pallas_call(
        kernel,
        out_shape=[jax.ShapeDtypeStruct((size, docs, blk), BF16)] * outs,
        in_specs=[SMEM] + [VMEM] * len(parts),
        out_specs=[VMEM] * outs,
        scratch_shapes=[pltpu.VMEM((blocks, docs, blk), F32)],
        name="add_blocks",
    )(index, *parts)


def residual_and_back(parts, weight, slot_position, order, positives, first_label):
    count = len(parts)
    cap, docs, blk = parts[0].shape
    label_blocks, slots = weight.shape[:2]
    uses = label_blocks * slots // (count * cap)
    pos_count = positives.shape[1]

    def kernel(position_ref, order_ref, first_ref, positives_ref, weight_hbm, *refs):
        ins = refs[:count]
        residual_ref = refs[count]
        outs = refs[count + 1 : 2 * count + 1]
        pool, weight_ref, pool_sem, weight_sem = refs[2 * count + 1 :]
        copies = [
            pltpu.make_async_copy(ins[q], pool.at[pl.ds(q * cap, cap)], pool_sem.at[q])
            for q in range(count)
        ]
        loads = [
            pltpu.make_async_copy(
                weight_hbm.at[g], weight_ref.at[pl.ds(g * slots, slots)], weight_sem.at[g]
            )
            for g in range(label_blocks)
        ]
        for copy in copies + loads:
            copy.start()
        for copy in copies:
            copy.wait()

        def forward(g, carry):
            pltpu.make_async_copy(
                weight_hbm.at[g], weight_ref.at[pl.ds(g * slots, slots)], weight_sem.at[g]
            ).wait()
            lhs = jnp.concatenate(
                [pool[position_ref[g * slots + s]] for s in range(slots)], axis=1
            )
            rhs = weight_ref[pl.ds(g * slots, slots)].reshape(slots * blk, blk)
            logits = jnp.dot(lhs, rhs, preferred_element_type=F32)
            ids = first_ref[0] + g * blk + lax.broadcasted_iota(jnp.int32, (docs, blk), 1)
            hit = positives_ref[:, 0:1] == ids
            for p in range(1, pos_count):
                hit = hit | (positives_ref[:, p : p + 1] == ids)
            residual_ref[g] = (jax.nn.sigmoid(logits) - jnp.where(hit, 1.0, 0.0)).astype(BF16)
            return carry

        lax.fori_loop(0, label_blocks, forward, 0, unroll=UNROLL)
        for q in range(count):

            def backward(k, carry):
                where = [order_ref[(q * cap + k) * uses + u] for u in range(uses)]
                lhs = jnp.concatenate([residual_ref[w // slots] for w in where], axis=1)
                rhs = jnp.concatenate([weight_ref[w] for w in where], axis=1)
                outs[q][k] = lax.dot_general(
                    lhs, rhs, (((1,), (1,)), ((), ())), preferred_element_type=F32
                ).astype(BF16)
                return carry

            lax.fori_loop(0, cap, backward, 0, unroll=2 * UNROLL)

    out = pl.pallas_call(
        kernel,
        out_shape=[jax.ShapeDtypeStruct((label_blocks, docs, blk), BF16)]
        + [jax.ShapeDtypeStruct((cap, docs, blk), BF16)] * count,
        in_specs=[SMEM] * 3 + [VMEM, ANY] + [VMEM] * count,
        out_specs=[VMEM] * (count + 1),
        scratch_shapes=[
            pltpu.VMEM((count * cap, docs, blk), BF16),
            pltpu.VMEM((label_blocks * slots, blk, blk), BF16),
            pltpu.SemaphoreType.DMA((count,)),
            pltpu.SemaphoreType.DMA((label_blocks,)),
        ],
        name="residual_and_back",
    )(slot_position, order, first_label, positives, weight, *parts)
    return out[0], list(out[1:])


def block_weight_grad(so_far, picked, residuals, order, label_blocks, slots):
    pieces = len(picked)
    cap, _, blk = picked[0].shape
    uses = order.shape[0] // cap
    earlier = [] if so_far is None else [so_far]

    def kernel(order_ref, *refs):
        residual_refs = refs[:pieces]
        ins = refs[pieces : 2 * pieces]
        out_ref, buffer, sem = refs[2 * pieces + len(earlier) :]

        def step(k, carry):
            where = [order_ref[k * uses + u] for u in range(uses)]
            rhs = jnp.concatenate(
                [
                    jnp.concatenate([ref[w // slots] for w in where], axis=1)
                    for ref in residual_refs
                ],
                axis=0,
            )
            lhs = jnp.concatenate([ref[k] for ref in ins], axis=0)
            out = lax.dot_general(
                lhs, rhs, (((0,), (0,)), ((), ())), preferred_element_type=F32
            ).astype(BF16)
            for u in range(uses):
                buffer[k * uses + u] = out[:, u * blk : (u + 1) * blk]
                pltpu.make_async_copy(buffer.at[k * uses + u], out_ref.at[where[u]], sem).start()
            return carry

        lax.fori_loop(0, cap, step, 0, unroll=UNROLL)
        pltpu.make_async_copy(buffer, out_ref.at[pl.ds(0, cap * uses)], sem).wait()

    return pl.pallas_call(
        kernel,
        out_shape=jax.ShapeDtypeStruct((label_blocks * slots, blk, blk), BF16),
        in_specs=[SMEM] + [VMEM] * (2 * pieces) + [ANY] * len(earlier),
        out_specs=ANY,
        input_output_aliases={1 + 2 * pieces: 0} if earlier else {},
        scratch_shapes=[pltpu.VMEM((cap * uses, blk, blk), BF16), pltpu.SemaphoreType.DMA(())],
        name="block_weight_grad",
    )(order, *residuals, *picked, *earlier)


def expand_weight_grad(documents, sides, columns, size, width):
    chunks = len(sides[0])
    pieces = sides[0][0].shape[0] // size
    blk = sides[0][0].shape[2]
    _, rows = documents.shape

    def kernel(columns_ref, documents_ref, *refs):
        out_ref = refs[-1]
        lhs = documents_ref[...]
        for i in range(len(sides) * pieces):
            ins = refs[i // pieces * chunks : (i // pieces + 1) * chunks]
            blocks = range(i % pieces * size, (i % pieces + 1) * size)
            rhs = jnp.concatenate(
                [jnp.concatenate([ref[j] for ref in ins], axis=0) for j in blocks], axis=1
            )
            out = lax.dot_general(
                lhs, rhs, (((0,), (0,)), ((), ())), preferred_element_type=F32
            )
            start = pl.multiple_of(columns_ref[i], blk)
            out_ref[:, pl.ds(start, size * blk)] = out.astype(BF16)

    return pl.pallas_call(
        kernel,
        out_shape=jax.ShapeDtypeStruct((rows, width), BF16),
        in_specs=[SMEM, VMEM] + [VMEM] * (len(sides) * chunks),
        out_specs=VMEM,
        name="expand_weight_grad",
    )(columns, documents, *[part for side in sides for part in side])


def list_tables(feature_lists, feat_index, label_index, label_count, own_count, label_blocks, cap):
    feat_count = lax.axis_size("feat")
    slots = feature_lists.shape[1]
    entries = label_blocks * slots
    ring = label_count // CORES
    own_blocks = own_count // label_count
    flips = jnp.arange(feat_count, dtype=jnp.int32)
    by_device = feature_lists.reshape(feat_count, label_count, entries)
    column = lax.dynamic_index_in_dim(by_device, label_index, 1, keepdims=False)
    mine = lax.dynamic_index_in_dim(column, feat_index, 0, keepdims=False)

    local = jnp.arange(own_count, dtype=jnp.int32)
    wanted = jnp.any(
        column[:, :, None] == (feat_index * own_count + local)[None, None, :], axis=1
    )
    rank = jnp.sum(wanted[:, None, :] & (local[None, :] < local[:, None])[None], axis=2)
    chosen = wanted[:, None, :] & (rank[:, None, :] == jnp.arange(cap)[None, :, None])
    ring_index, core = label_index // CORES, label_index % CORES
    owner_ring = local // (CORES * own_blocks)
    owner_core = local // own_blocks % CORES
    place = (
        jnp.where(owner_core == core, 0, ring) + (owner_ring ^ ring_index)
    ) * own_blocks + local % own_blocks
    send = jnp.sum(jnp.where(chosen, place[None, None, :], 0), axis=2).astype(jnp.int32)
    send = jnp.stack(
        [lax.dynamic_index_in_dim(send, feat_index ^ m, 0, keepdims=False) for m in range(feat_count)]
    ).reshape(-1)

    block = jnp.arange(feat_count * own_count, dtype=jnp.int32)
    present = jnp.any(mine[:, None] == block[None, :], axis=0)
    before = jnp.sum(
        present[None, :]
        & (block[None, :] // own_count == block[:, None] // own_count)
        & (block[None, :] < block[:, None]),
        axis=1,
    )
    table = ((block // own_count) ^ feat_index) * cap + before
    position = jnp.sum(
        jnp.where(mine[:, None] == block[None, :], table[None, :], 0), axis=1
    ).astype(jnp.int32)
    entry = jnp.arange(entries, dtype=jnp.int32)
    earlier = jnp.sum((mine[None, :] == mine[:, None]) & (entry[None, :] < entry[:, None]), axis=1)
    uses = entries // (feat_count * cap)
    key = position * uses + earlier
    order = jnp.sum(jnp.where(key[None, :] == entry[:, None], entry[None, :], 0), axis=1)
    return send, position, order.astype(jnp.int32)


def program(documents, expand_weight, sparse_weight, feature_lists, positives):
    feat_count = lax.axis_size("feat")
    label_count = lax.axis_size("label")
    feat_index = lax.axis_index("feat")
    label_index = lax.axis_index("label")
    group = feat_index * label_count + label_index
    ring = label_count // CORES
    ring_index, core = label_index // CORES, label_index % CORES
    docs = documents.shape[0]
    _, width = expand_weight.shape
    own_count = width // BLK
    own_blocks = own_count // label_count
    label_blocks, slots = sparse_weight.shape[:2]
    cap = CAP
    chunk = docs // CHUNKS
    cuts = [slice(i * chunk, (i + 1) * chunk) for i in range(CHUNKS)]

    ring_width = width // ring
    starts = (jnp.arange(ring, dtype=jnp.int32) ^ ring_index) * ring_width

    def product(left, right):
        right = right.reshape(right.shape[0], ring_width // BLK, BLK)
        return jnp.einsum("dk,kbc->bdc", left, right, preferred_element_type=F32)

    columns = cut_columns(expand_weight, starts, ring_width)
    arrived = [columns[0]] + [None] * (ring - 1)
    for k in range(ring - 1, 0, -1):
        arrived[k] = ring_exchange(columns[k], k)
    documents_late, _ = lax.optimization_barrier((documents, columns[0]))
    expanded = product(documents, columns[0])
    for k in range(1, ring):
        other = ring_exchange(documents_late, k)
        expanded = expanded + product(other, arrived[k])
    kept = lax.dynamic_slice_in_dim(expanded, core * own_blocks, own_blocks, 0)
    given = lax.dynamic_slice_in_dim(expanded, (1 - core) * own_blocks, own_blocks, 0)

    send, position, order = list_tables(
        feature_lists, feat_index, label_index, label_count, own_count, label_blocks, cap
    )
    first_label = (group * label_blocks * BLK).reshape(1)
    known = [positives[cut] for cut in cuts]
    given, send, position, order, known, first_label = lax.optimization_barrier(
        (given, send, position, order, known, first_label)
    )
    hidden = jnp.maximum(kept + swap_cores(given), 0.0).astype(BF16)

    picked, residuals, gradients = [], [], []
    for i, cut in enumerate(cuts):
        pool = jnp.concatenate(ring_gather(hidden[:, cut]), axis=0)
        pools = [pool, swap_cores(pool)]
        outgoing = select_blocks(pools, send, cap)
        parts = [outgoing[0]] + [None] * (feat_count - 1)
        for m in range(feat_count - 1, 0, -1):
            parts[m] = feat_exchange(outgoing[m], m)
        residual, back = residual_and_back(
            parts, sparse_weight, position, order, known[i], first_label
        )
        picked.append(parts)
        residuals.append(residual)
        returned = [back[0]] + [None] * (feat_count - 1)
        for m in range(feat_count - 1, 0, -1):
            returned[m] = feat_exchange(back[m], m)
        kept, given = add_blocks(returned, send, own_count, CORES)
        both = (kept.astype(F32) + swap_cores(given).astype(F32)).astype(BF16)
        pieces = [both[k * own_blocks : (k + 1) * own_blocks] for k in range(ring)]
        total = pieces[0].astype(F32)
        for k in range(ring - 1, 0, -1):
            total = total + ring_exchange(pieces[k], k).astype(F32)
        if gradients:
            total, _ = lax.optimization_barrier((total, gradients[-1][0]))
        gradient = jnp.where(hidden[:, cut] > 0, total, 0.0).astype(BF16)
        gathered = jnp.concatenate(ring_gather(gradient), axis=0)
        gradients.append((gathered, swap_cores(gathered)))

    grad_sparse = None
    share = order.shape[0] // feat_count
    for m in range(feat_count):
        grad_sparse = block_weight_grad(
            grad_sparse,
            [parts[m] for parts in picked],
            residuals,
            order[m * share : (m + 1) * share],
            label_blocks,
            slots,
        )
    grad_sparse = grad_sparse.reshape(sparse_weight.shape)

    places = jnp.arange(CORES * ring, dtype=jnp.int32)
    owners = ((places % ring) ^ ring_index) * CORES + (places // ring ^ core)
    sides = [[gradient[side] for gradient in gradients] for side in range(CORES)]
    grad_expand = expand_weight_grad(
        documents, sides, owners * (own_blocks * BLK), own_blocks, width
    )
    return (grad_expand, grad_sparse)


def solution(mesh):
    return jax.shard_map(
        program,
        mesh=mesh,
        in_specs=(
            P(None, "label"),
            P("label", "feat"),
            P(("feat", "label"), None, None, None),
            P(),
            P(),
        ),
        out_specs=(P("label", "feat"), P(("feat", "label"), None, None, None)),
        check_vma=False,
    )
```

```python
import math

import jax
import jax.numpy as jnp
from jax import lax
from jax.experimental import pallas as pl
from jax.experimental.pallas import tpu as pltpu
from jax.sharding import PartitionSpec as P


BLK = 128
CAP = 24
CORES = 2
CHUNKS = 2
UNROLL = 4
SPARE_BYTES = 2 << 20

BF16 = jnp.bfloat16
F32 = jnp.float32
VMEM = pl.BlockSpec(memory_space=pltpu.VMEM)
SMEM = pl.BlockSpec(memory_space=pltpu.SMEM)
ANY = pl.BlockSpec(memory_space=pl.ANY)


def ring_exchange(x, flip):
    count = lax.axis_size("label")
    return lax.ppermute(x, "label", [(i, i ^ (flip * CORES)) for i in range(count)])


def swap_cores(x):
    count = lax.axis_size("label")
    return lax.ppermute(x, "label", [(i, i ^ 1) for i in range(count)])


def feat_exchange(x, flip):
    return lax.ppermute(x, "feat", [(i, i ^ flip) for i in range(lax.axis_size("feat"))])


def ring_gather(own):
    ring = lax.axis_size("label") // CORES
    return [own] + [ring_exchange(own, k) for k in range(1, ring)]


def grant(*blocks):
    total = 0
    for shape, dtype in blocks:
        total += math.prod(shape) * jnp.dtype(dtype).itemsize
    return pltpu.CompilerParams(vmem_limit_bytes=total + total // 8 + SPARE_BYTES)


def blocks_of(arrays):
    return [(x.shape, x.dtype) for x in arrays]


def cut_columns(weight, starts, width):
    count = starts.shape[0]

    def kernel(starts_ref, weight_ref, *outs):
        for k, out in enumerate(outs):
            out[...] = weight_ref[:, pl.ds(pl.multiple_of(starts_ref[k], BLK), width)]

    return pl.pallas_call(
        kernel,
        out_shape=[jax.ShapeDtypeStruct((weight.shape[0], width), weight.dtype)] * count,
        in_specs=[SMEM, VMEM],
        out_specs=[VMEM] * count,
        compiler_params=grant((weight.shape, BF16), (weight.shape, BF16)),
        name="cut_columns",
    )(starts, weight)


def fetch(array):
    def kernel(source, target, sem):
        copy = pltpu.make_async_copy(source, target, sem)
        copy.start()
        copy.wait()

    return pl.pallas_call(
        kernel,
        out_shape=jax.ShapeDtypeStruct(array.shape, array.dtype),
        in_specs=[pl.BlockSpec(memory_space=pltpu.HBM)],
        out_specs=VMEM,
        scratch_shapes=[pltpu.SemaphoreType.DMA(())],
        compiler_params=grant((array.shape, array.dtype)),
        name="fetch",
    )(pltpu.with_memory_space_constraint(array, pltpu.HBM))


def select_blocks(pools, index, cap):
    size, docs, blk = pools[0].shape
    outs = index.shape[0] // cap

    def kernel(index_ref, *refs):
        ins = refs[: len(pools)]
        out_refs = refs[len(pools) :]
        for m in range(outs):

            def step(k, carry):
                place = index_ref[m * cap + k]
                block = ins[0][place % size]
                for i in range(1, len(ins)):
                    block = jnp.where(place >= i * size, ins[i][place % size], block)
                out_refs[m][k] = block
                return carry

            lax.fori_loop(0, cap, step, 0, unroll=UNROLL)

    return pl.pallas_call(
        kernel,
        out_shape=[jax.ShapeDtypeStruct((cap, docs, blk), BF16)] * outs,
        in_specs=[SMEM] + [VMEM] * len(pools),
        out_specs=[VMEM] * outs,
        compiler_params=grant(*blocks_of(pools), ((outs * cap, docs, blk), BF16)),
        name="select_blocks",
    )(index, *pools)


def add_blocks(parts, index, blocks, outs):
    cap, docs, blk = parts[0].shape
    size = blocks // outs

    def kernel(index_ref, *refs):
        ins = refs[: len(parts)]
        out_refs = refs[len(parts) : len(parts) + outs]
        total = refs[-1]
        total[...] = jnp.zeros_like(total)
        for m, ref in enumerate(ins):

            def step(k, carry):
                total[index_ref[m * cap + k]] += ref[k].astype(F32)
                return carry

            lax.fori_loop(0, cap, step, 0, unroll=UNROLL)
        for i, ref in enumerate(out_refs):
            ref[...] = total[pl.ds(i * size, size)].astype(BF16)

    return pl.pallas_call(
        kernel,
        out_shape=[jax.ShapeDtypeStruct((size, docs, blk), BF16)] * outs,
        in_specs=[SMEM] + [VMEM] * len(parts),
        out_specs=[VMEM] * outs,
        scratch_shapes=[pltpu.VMEM((blocks, docs, blk), F32)],
        compiler_params=grant(
            *blocks_of(parts), ((blocks, docs, blk), F32), ((blocks, docs, blk), BF16)
        ),
        name="add_blocks",
    )(index, *parts)


def residual_and_back(parts, weight, slot_position, order, positives, first_label):
    count = len(parts)
    cap, docs, blk = parts[0].shape
    label_blocks, slots = weight.shape[:2]
    uses = label_blocks * slots // (count * cap)
    pos_count = positives.shape[1]

    def kernel(position_ref, order_ref, first_ref, positives_ref, weight_ref, *refs):
        ins = refs[:count]
        residual_ref = refs[count]
        outs = refs[count + 1 : 2 * count + 1]
        pool, pool_sem = refs[2 * count + 1 :]
        copies = [
            pltpu.make_async_copy(ins[q], pool.at[pl.ds(q * cap, cap)], pool_sem.at[q])
            for q in range(count)
        ]
        for copy in copies:
            copy.start()
        for copy in copies:
            copy.wait()

        def forward(g, carry):
            lhs = jnp.concatenate(
                [pool[position_ref[g * slots + s]] for s in range(slots)], axis=1
            )
            rhs = weight_ref[g].reshape(slots * blk, blk)
            logits = jnp.dot(lhs, rhs, preferred_element_type=F32)
            ids = first_ref[0] + g * blk + lax.broadcasted_iota(jnp.int32, (docs, blk), 1)
            hit = positives_ref[:, 0:1] == ids
            for p in range(1, pos_count):
                hit = hit | (positives_ref[:, p : p + 1] == ids)
            residual_ref[g] = (jax.nn.sigmoid(logits) - jnp.where(hit, 1.0, 0.0)).astype(BF16)
            return carry

        lax.fori_loop(0, label_blocks, forward, 0, unroll=UNROLL)
        for q in range(count):

            def backward(k, carry):
                where = [order_ref[(q * cap + k) * uses + u] for u in range(uses)]
                lhs = jnp.concatenate([residual_ref[w // slots] for w in where], axis=1)
                rhs = jnp.concatenate([weight_ref[w // slots, w % slots] for w in where], axis=1)
                outs[q][k] = lax.dot_general(
                    lhs, rhs, (((1,), (1,)), ((), ())), preferred_element_type=F32
                ).astype(BF16)
                return carry

            lax.fori_loop(0, cap, backward, 0, unroll=2 * UNROLL)

    out = pl.pallas_call(
        kernel,
        out_shape=[jax.ShapeDtypeStruct((label_blocks, docs, blk), BF16)]
        + [jax.ShapeDtypeStruct((cap, docs, blk), BF16)] * count,
        in_specs=[SMEM] * 3 + [VMEM] * (2 + count),
        out_specs=[VMEM] * (count + 1),
        scratch_shapes=[
            pltpu.VMEM((count * cap, docs, blk), BF16),
            pltpu.SemaphoreType.DMA((count,)),
        ],
        compiler_params=grant(
            (weight.shape, BF16),
            ((3 * count * cap, docs, blk), BF16),
            ((label_blocks, docs, blk), BF16),
        ),
        name="residual_and_back",
    )(slot_position, order, first_label, positives, weight, *parts)
    return out[0], list(out[1:])


def block_weight_grad(so_far, picked, residuals, order, label_blocks, slots):
    pieces = len(picked)
    cap, _, blk = picked[0].shape
    uses = order.shape[0] // cap
    earlier = [] if so_far is None else [so_far]

    def kernel(order_ref, *refs):
        residual_refs = refs[:pieces]
        ins = refs[pieces : 2 * pieces]
        out_ref, buffer, sem = refs[2 * pieces + len(earlier) :]

        def step(k, carry):
            where = [order_ref[k * uses + u] for u in range(uses)]
            rhs = jnp.concatenate(
                [
                    jnp.concatenate([ref[w // slots] for w in where], axis=1)
                    for ref in residual_refs
                ],
                axis=0,
            )
            lhs = jnp.concatenate([ref[k] for ref in ins], axis=0)
            out = lax.dot_general(
                lhs, rhs, (((0,), (0,)), ((), ())), preferred_element_type=F32
            ).astype(BF16)
            for u in range(uses):
                buffer[k * uses + u] = out[:, u * blk : (u + 1) * blk]
                pltpu.make_async_copy(buffer.at[k * uses + u], out_ref.at[where[u]], sem).start()
            return carry

        lax.fori_loop(0, cap, step, 0, unroll=UNROLL)
        pltpu.make_async_copy(buffer, out_ref.at[pl.ds(0, cap * uses)], sem).wait()

    return pl.pallas_call(
        kernel,
        out_shape=jax.ShapeDtypeStruct((label_blocks * slots, blk, blk), BF16),
        in_specs=[SMEM] + [VMEM] * (2 * pieces) + [ANY] * len(earlier),
        out_specs=ANY,
        input_output_aliases={1 + 2 * pieces: 0} if earlier else {},
        scratch_shapes=[pltpu.VMEM((cap * uses, blk, blk), BF16), pltpu.SemaphoreType.DMA(())],
        compiler_params=grant(
            ((cap * uses, blk, blk), BF16), *blocks_of(picked), *blocks_of(residuals)
        ),
        name="block_weight_grad",
    )(order, *residuals, *picked, *earlier)


def expand_weight_grad(documents, sides, columns, size, width):
    chunks = len(sides[0])
    pieces = sides[0][0].shape[0] // size
    blk = sides[0][0].shape[2]
    _, rows = documents.shape

    def kernel(columns_ref, documents_ref, *refs):
        out_ref = refs[-1]
        lhs = documents_ref[...]
        for i in range(len(sides) * pieces):
            ins = refs[i // pieces * chunks : (i // pieces + 1) * chunks]
            blocks = range(i % pieces * size, (i % pieces + 1) * size)
            rhs = jnp.concatenate(
                [jnp.concatenate([ref[j] for ref in ins], axis=0) for j in blocks], axis=1
            )
            out = lax.dot_general(
                lhs, rhs, (((0,), (0,)), ((), ())), preferred_element_type=F32
            )
            start = pl.multiple_of(columns_ref[i], blk)
            out_ref[:, pl.ds(start, size * blk)] = out.astype(BF16)

    return pl.pallas_call(
        kernel,
        out_shape=jax.ShapeDtypeStruct((rows, width), BF16),
        in_specs=[SMEM, VMEM] + [VMEM] * (len(sides) * chunks),
        out_specs=VMEM,
        compiler_params=grant(
            ((rows, width), BF16), ((rows, width), F32), *blocks_of(sum(sides, []))
        ),
        name="expand_weight_grad",
    )(columns, documents, *[part for side in sides for part in side])


def list_tables(feature_lists, feat_index, label_index, label_count, own_count, label_blocks, cap):
    feat_count = lax.axis_size("feat")
    slots = feature_lists.shape[1]
    entries = label_blocks * slots
    ring = label_count // CORES
    own_blocks = own_count // label_count
    flips = jnp.arange(feat_count, dtype=jnp.int32)
    by_device = feature_lists.reshape(feat_count, label_count, entries)
    column = lax.dynamic_index_in_dim(by_device, label_index, 1, keepdims=False)
    mine = lax.dynamic_index_in_dim(column, feat_index, 0, keepdims=False)

    local = jnp.arange(own_count, dtype=jnp.int32)
    wanted = jnp.any(
        column[:, :, None] == (feat_index * own_count + local)[None, None, :], axis=1
    )
    rank = jnp.sum(wanted[:, None, :] & (local[None, :] < local[:, None])[None], axis=2)
    chosen = wanted[:, None, :] & (rank[:, None, :] == jnp.arange(cap)[None, :, None])
    ring_index, core = label_index // CORES, label_index % CORES
    owner_ring = local // (CORES * own_blocks)
    owner_core = local // own_blocks % CORES
    place = (
        jnp.where(owner_core == core, 0, ring) + (owner_ring ^ ring_index)
    ) * own_blocks + local % own_blocks
    send = jnp.sum(jnp.where(chosen, place[None, None, :], 0), axis=2).astype(jnp.int32)
    send = jnp.stack(
        [lax.dynamic_index_in_dim(send, feat_index ^ m, 0, keepdims=False) for m in range(feat_count)]
    ).reshape(-1)

    block = jnp.arange(feat_count * own_count, dtype=jnp.int32)
    present = jnp.any(mine[:, None] == block[None, :], axis=0)
    before = jnp.sum(
        present[None, :]
        & (block[None, :] // own_count == block[:, None] // own_count)
        & (block[None, :] < block[:, None]),
        axis=1,
    )
    table = ((block // own_count) ^ feat_index) * cap + before
    position = jnp.sum(
        jnp.where(mine[:, None] == block[None, :], table[None, :], 0), axis=1
    ).astype(jnp.int32)
    entry = jnp.arange(entries, dtype=jnp.int32)
    earlier = jnp.sum((mine[None, :] == mine[:, None]) & (entry[None, :] < entry[:, None]), axis=1)
    uses = entries // (feat_count * cap)
    key = position * uses + earlier
    order = jnp.sum(jnp.where(key[None, :] == entry[:, None], entry[None, :], 0), axis=1)
    return send, position, order.astype(jnp.int32)


def program(documents, expand_weight, sparse_weight, feature_lists, positives):
    feat_count = lax.axis_size("feat")
    label_count = lax.axis_size("label")
    feat_index = lax.axis_index("feat")
    label_index = lax.axis_index("label")
    group = feat_index * label_count + label_index
    ring = label_count // CORES
    ring_index, core = label_index // CORES, label_index % CORES
    docs = documents.shape[0]
    _, width = expand_weight.shape
    own_count = width // BLK
    own_blocks = own_count // label_count
    label_blocks, slots = sparse_weight.shape[:2]
    cap = CAP
    chunk = docs // CHUNKS
    cuts = [slice(i * chunk, (i + 1) * chunk) for i in range(CHUNKS)]

    ring_width = width // ring
    starts = (jnp.arange(ring, dtype=jnp.int32) ^ ring_index) * ring_width

    def product(left, right):
        right = right.reshape(right.shape[0], ring_width // BLK, BLK)
        return jnp.einsum("dk,kbc->bdc", left, right, preferred_element_type=F32)

    columns = cut_columns(expand_weight, starts, ring_width)
    arrived = [columns[0]] + [None] * (ring - 1)
    for k in range(ring - 1, 0, -1):
        arrived[k] = ring_exchange(columns[k], k)
    documents_late, _ = lax.optimization_barrier((documents, columns[0]))
    expanded = product(documents, columns[0])
    for k in range(1, ring):
        other = ring_exchange(documents_late, k)
        expanded = expanded + product(other, arrived[k])
    kept = lax.dynamic_slice_in_dim(expanded, core * own_blocks, own_blocks, 0)
    given = lax.dynamic_slice_in_dim(expanded, (1 - core) * own_blocks, own_blocks, 0)

    block_weight = fetch(sparse_weight)
    send, position, order = list_tables(
        feature_lists, feat_index, label_index, label_count, own_count, label_blocks, cap
    )
    first_label = (group * label_blocks * BLK).reshape(1)
    known = [positives[cut] for cut in cuts]
    given, send, position, order, known, first_label = lax.optimization_barrier(
        (given, send, position, order, known, first_label)
    )
    hidden = jnp.maximum(kept + swap_cores(given), 0.0).astype(BF16)

    picked, residuals, gradients = [], [], []
    for i, cut in enumerate(cuts):
        pool = jnp.concatenate(ring_gather(hidden[:, cut]), axis=0)
        pools = [pool, swap_cores(pool)]
        outgoing = select_blocks(pools, send, cap)
        parts = [outgoing[0]] + [None] * (feat_count - 1)
        for m in range(feat_count - 1, 0, -1):
            parts[m] = feat_exchange(outgoing[m], m)
        residual, back = residual_and_back(
            parts, block_weight, position, order, known[i], first_label
        )
        picked.append(parts)
        residuals.append(residual)
        returned = [back[0]] + [None] * (feat_count - 1)
        for m in range(feat_count - 1, 0, -1):
            returned[m] = feat_exchange(back[m], m)
        kept, given = add_blocks(returned, send, own_count, CORES)
        both = (kept.astype(F32) + swap_cores(given).astype(F32)).astype(BF16)
        pieces = [both[k * own_blocks : (k + 1) * own_blocks] for k in range(ring)]
        total = pieces[0].astype(F32)
        for k in range(ring - 1, 0, -1):
            total = total + ring_exchange(pieces[k], k).astype(F32)
        if gradients:
            total, _ = lax.optimization_barrier((total, gradients[-1][0]))
        gradient = jnp.where(hidden[:, cut] > 0, total, 0.0).astype(BF16)
        gathered = jnp.concatenate(ring_gather(gradient), axis=0)
        gradients.append((gathered, swap_cores(gathered)))

    grad_sparse = None
    share = order.shape[0] // feat_count
    for m in range(feat_count):
        grad_sparse = block_weight_grad(
            grad_sparse,
            [parts[m] for parts in picked],
            residuals,
            order[m * share : (m + 1) * share],
            label_blocks,
            slots,
        )
    grad_sparse = grad_sparse.reshape(sparse_weight.shape)

    places = jnp.arange(CORES * ring, dtype=jnp.int32)
    owners = ((places % ring) ^ ring_index) * CORES + (places // ring ^ core)
    sides = [[gradient[side] for gradient in gradients] for side in range(CORES)]
    grad_expand = expand_weight_grad(
        documents, sides, owners * (own_blocks * BLK), own_blocks, width
    )
    return (grad_expand, grad_sparse)


def solution(mesh):
    return jax.shard_map(
        program,
        mesh=mesh,
        in_specs=(
            P(None, "label"),
            P("label", "feat"),
            P(("feat", "label"), None, None, None),
            P(),
            P(),
        ),
        out_specs=(P("label", "feat"), P(("feat", "label"), None, None, None)),
        check_vma=False,
    )
```

```python
import math

import jax
import jax.numpy as jnp
from jax import lax
from jax.experimental import pallas as pl
from jax.experimental.pallas import tpu as pltpu
from jax.sharding import PartitionSpec as P


BLK = 128
CAP = 24
CORES = 2
CHUNK_TENTHS = (3, 4, 3)
UNROLL = 4
SPARE_BYTES = 2 << 20

BF16 = jnp.bfloat16
F32 = jnp.float32
VMEM = pl.BlockSpec(memory_space=pltpu.VMEM)
SMEM = pl.BlockSpec(memory_space=pltpu.SMEM)
ANY = pl.BlockSpec(memory_space=pl.ANY)


def ring_exchange(x, flip):
    count = lax.axis_size("label")
    return lax.ppermute(x, "label", [(i, i ^ (flip * CORES)) for i in range(count)])


def swap_cores(x):
    count = lax.axis_size("label")
    return lax.ppermute(x, "label", [(i, i ^ 1) for i in range(count)])


def feat_exchange(x, flip):
    return lax.ppermute(x, "feat", [(i, i ^ flip) for i in range(lax.axis_size("feat"))])


def ring_gather(own):
    ring = lax.axis_size("label") // CORES
    return [own] + [ring_exchange(own, k) for k in range(1, ring)]


def grant(*blocks):
    total = 0
    for shape, dtype in blocks:
        total += math.prod(shape) * jnp.dtype(dtype).itemsize
    return pltpu.CompilerParams(vmem_limit_bytes=total + total // 8 + SPARE_BYTES)


def blocks_of(arrays):
    return [(x.shape, x.dtype) for x in arrays]


def cut_columns(weight, starts, width):
    count = starts.shape[0]

    def kernel(starts_ref, weight_ref, *outs):
        for k, out in enumerate(outs):
            out[...] = weight_ref[:, pl.ds(pl.multiple_of(starts_ref[k], BLK), width)]

    return pl.pallas_call(
        kernel,
        out_shape=[jax.ShapeDtypeStruct((weight.shape[0], width), weight.dtype)] * count,
        in_specs=[SMEM, VMEM],
        out_specs=[VMEM] * count,
        compiler_params=grant((weight.shape, BF16), (weight.shape, BF16)),
        name="cut_columns",
    )(starts, weight)


def fetch(array):
    def kernel(source, target, sem):
        copy = pltpu.make_async_copy(source, target, sem)
        copy.start()
        copy.wait()

    return pl.pallas_call(
        kernel,
        out_shape=jax.ShapeDtypeStruct(array.shape, array.dtype),
        in_specs=[pl.BlockSpec(memory_space=pltpu.HBM)],
        out_specs=VMEM,
        scratch_shapes=[pltpu.SemaphoreType.DMA(())],
        compiler_params=grant((array.shape, array.dtype)),
        name="fetch",
    )(pltpu.with_memory_space_constraint(array, pltpu.HBM))


def select_blocks(pools, index, cap):
    size, docs, blk = pools[0].shape
    outs = index.shape[0] // cap

    def kernel(index_ref, *refs):
        ins = refs[: len(pools)]
        out_refs = refs[len(pools) :]
        for m in range(outs):

            def step(k, carry):
                place = index_ref[m * cap + k]
                block = ins[0][place % size]
                for i in range(1, len(ins)):
                    block = jnp.where(place >= i * size, ins[i][place % size], block)
                out_refs[m][k] = block
                return carry

            lax.fori_loop(0, cap, step, 0, unroll=UNROLL)

    return pl.pallas_call(
        kernel,
        out_shape=[jax.ShapeDtypeStruct((cap, docs, blk), BF16)] * outs,
        in_specs=[SMEM] + [VMEM] * len(pools),
        out_specs=[VMEM] * outs,
        compiler_params=grant(*blocks_of(pools), ((outs * cap, docs, blk), BF16)),
        name="select_blocks",
    )(index, *pools)


def add_blocks(parts, index, blocks, outs):
    cap, docs, blk = parts[0].shape
    size = blocks // outs

    def kernel(index_ref, *refs):
        ins = refs[: len(parts)]
        out_refs = refs[len(parts) : len(parts) + outs]
        total = refs[-1]
        total[...] = jnp.zeros_like(total)
        for m, ref in enumerate(ins):

            def step(k, carry):
                total[index_ref[m * cap + k]] += ref[k].astype(F32)
                return carry

            lax.fori_loop(0, cap, step, 0, unroll=UNROLL)
        for i, ref in enumerate(out_refs):
            ref[...] = total[pl.ds(i * size, size)].astype(BF16)

    return pl.pallas_call(
        kernel,
        out_shape=[jax.ShapeDtypeStruct((size, docs, blk), BF16)] * outs,
        in_specs=[SMEM] + [VMEM] * len(parts),
        out_specs=[VMEM] * outs,
        scratch_shapes=[pltpu.VMEM((blocks, docs, blk), F32)],
        compiler_params=grant(
            *blocks_of(parts), ((blocks, docs, blk), F32), ((blocks, docs, blk), BF16)
        ),
        name="add_blocks",
    )(index, *parts)


def residual_and_back(parts, weight, slot_position, order, positives, first_label):
    count = len(parts)
    cap, docs, blk = parts[0].shape
    label_blocks, slots = weight.shape[:2]
    uses = label_blocks * slots // (count * cap)
    pos_count = positives.shape[1]

    def kernel(position_ref, order_ref, first_ref, positives_ref, weight_ref, *refs):
        ins = refs[:count]
        residual_ref = refs[count]
        outs = refs[count + 1 : 2 * count + 1]
        pool, pool_sem = refs[2 * count + 1 :]
        copies = [
            pltpu.make_async_copy(ins[q], pool.at[pl.ds(q * cap, cap)], pool_sem.at[q])
            for q in range(count)
        ]
        for copy in copies:
            copy.start()
        for copy in copies:
            copy.wait()

        def forward(g, carry):
            lhs = jnp.concatenate(
                [pool[position_ref[g * slots + s]] for s in range(slots)], axis=1
            )
            rhs = weight_ref[g].reshape(slots * blk, blk)
            logits = jnp.dot(lhs, rhs, preferred_element_type=F32)
            ids = first_ref[0] + g * blk + lax.broadcasted_iota(jnp.int32, (docs, blk), 1)
            hit = positives_ref[:, 0:1] == ids
            for p in range(1, pos_count):
                hit = hit | (positives_ref[:, p : p + 1] == ids)
            residual_ref[g] = (jax.nn.sigmoid(logits) - jnp.where(hit, 1.0, 0.0)).astype(BF16)
            return carry

        lax.fori_loop(0, label_blocks, forward, 0, unroll=UNROLL)
        for q in range(count):

            def backward(k, carry):
                where = [order_ref[(q * cap + k) * uses + u] for u in range(uses)]
                lhs = jnp.concatenate([residual_ref[w // slots] for w in where], axis=1)
                rhs = jnp.concatenate([weight_ref[w // slots, w % slots] for w in where], axis=1)
                outs[q][k] = lax.dot_general(
                    lhs, rhs, (((1,), (1,)), ((), ())), preferred_element_type=F32
                ).astype(BF16)
                return carry

            lax.fori_loop(0, cap, backward, 0, unroll=2 * UNROLL)

    out = pl.pallas_call(
        kernel,
        out_shape=[jax.ShapeDtypeStruct((label_blocks, docs, blk), BF16)]
        + [jax.ShapeDtypeStruct((cap, docs, blk), BF16)] * count,
        in_specs=[SMEM] * 3 + [VMEM] * (2 + count),
        out_specs=[VMEM] * (count + 1),
        scratch_shapes=[
            pltpu.VMEM((count * cap, docs, blk), BF16),
            pltpu.SemaphoreType.DMA((count,)),
        ],
        compiler_params=grant(
            (weight.shape, BF16),
            ((3 * count * cap, docs, blk), BF16),
            ((label_blocks, docs, blk), BF16),
        ),
        name="residual_and_back",
    )(slot_position, order, first_label, positives, weight, *parts)
    return out[0], list(out[1:])


def block_weight_grad(so_far, picked, residuals, order, label_blocks, slots):
    pieces = len(picked)
    cap, _, blk = picked[0].shape
    uses = order.shape[0] // cap
    earlier = [] if so_far is None else [so_far]

    def kernel(order_ref, *refs):
        residual_refs = refs[:pieces]
        ins = refs[pieces : 2 * pieces]
        out_ref, buffer, sem = refs[2 * pieces + len(earlier) :]

        def step(k, carry):
            where = [order_ref[k * uses + u] for u in range(uses)]
            rhs = jnp.concatenate(
                [
                    jnp.concatenate([ref[w // slots] for w in where], axis=1)
                    for ref in residual_refs
                ],
                axis=0,
            )
            lhs = jnp.concatenate([ref[k] for ref in ins], axis=0)
            out = lax.dot_general(
                lhs, rhs, (((0,), (0,)), ((), ())), preferred_element_type=F32
            ).astype(BF16)
            for u in range(uses):
                buffer[k * uses + u] = out[:, u * blk : (u + 1) * blk]
                pltpu.make_async_copy(buffer.at[k * uses + u], out_ref.at[where[u]], sem).start()
            return carry

        lax.fori_loop(0, cap, step, 0, unroll=UNROLL)
        pltpu.make_async_copy(buffer, out_ref.at[pl.ds(0, cap * uses)], sem).wait()

    return pl.pallas_call(
        kernel,
        out_shape=jax.ShapeDtypeStruct((label_blocks * slots, blk, blk), BF16),
        in_specs=[SMEM] + [VMEM] * (2 * pieces) + [ANY] * len(earlier),
        out_specs=ANY,
        input_output_aliases={1 + 2 * pieces: 0} if earlier else {},
        scratch_shapes=[pltpu.VMEM((cap * uses, blk, blk), BF16), pltpu.SemaphoreType.DMA(())],
        compiler_params=grant(
            ((cap * uses, blk, blk), BF16), *blocks_of(picked), *blocks_of(residuals)
        ),
        name="block_weight_grad",
    )(order, *residuals, *picked, *earlier)


def expand_weight_grad(documents, sides, columns, size, width):
    chunks = len(sides[0])
    pieces = sides[0][0].shape[0] // size
    blk = sides[0][0].shape[2]
    _, rows = documents.shape

    def kernel(columns_ref, documents_ref, *refs):
        out_ref = refs[-1]
        lhs = documents_ref[...]
        for i in range(len(sides) * pieces):
            ins = refs[i // pieces * chunks : (i // pieces + 1) * chunks]
            blocks = range(i % pieces * size, (i % pieces + 1) * size)
            rhs = jnp.concatenate(
                [jnp.concatenate([ref[j] for ref in ins], axis=0) for j in blocks], axis=1
            )
            out = lax.dot_general(
                lhs, rhs, (((0,), (0,)), ((), ())), preferred_element_type=F32
            )
            start = pl.multiple_of(columns_ref[i], blk)
            out_ref[:, pl.ds(start, size * blk)] = out.astype(BF16)

    return pl.pallas_call(
        kernel,
        out_shape=jax.ShapeDtypeStruct((rows, width), BF16),
        in_specs=[SMEM, VMEM] + [VMEM] * (len(sides) * chunks),
        out_specs=VMEM,
        compiler_params=grant(
            ((rows, width), BF16), ((rows, width), F32), *blocks_of(sum(sides, []))
        ),
        name="expand_weight_grad",
    )(columns, documents, *[part for side in sides for part in side])


def list_tables(feature_lists, feat_index, label_index, label_count, own_count, label_blocks, cap):
    feat_count = lax.axis_size("feat")
    slots = feature_lists.shape[1]
    entries = label_blocks * slots
    ring = label_count // CORES
    own_blocks = own_count // label_count
    flips = jnp.arange(feat_count, dtype=jnp.int32)
    by_device = feature_lists.reshape(feat_count, label_count, entries)
    column = lax.dynamic_index_in_dim(by_device, label_index, 1, keepdims=False)
    mine = lax.dynamic_index_in_dim(column, feat_index, 0, keepdims=False)

    local = jnp.arange(own_count, dtype=jnp.int32)
    wanted = jnp.any(
        column[:, :, None] == (feat_index * own_count + local)[None, None, :], axis=1
    )
    rank = jnp.sum(wanted[:, None, :] & (local[None, :] < local[:, None])[None], axis=2)
    chosen = wanted[:, None, :] & (rank[:, None, :] == jnp.arange(cap)[None, :, None])
    ring_index, core = label_index // CORES, label_index % CORES
    owner_ring = local // (CORES * own_blocks)
    owner_core = local // own_blocks % CORES
    place = (
        jnp.where(owner_core == core, 0, ring) + (owner_ring ^ ring_index)
    ) * own_blocks + local % own_blocks
    send = jnp.sum(jnp.where(chosen, place[None, None, :], 0), axis=2).astype(jnp.int32)
    send = jnp.stack(
        [lax.dynamic_index_in_dim(send, feat_index ^ m, 0, keepdims=False) for m in range(feat_count)]
    ).reshape(-1)

    block = jnp.arange(feat_count * own_count, dtype=jnp.int32)
    present = jnp.any(mine[:, None] == block[None, :], axis=0)
    before = jnp.sum(
        present[None, :]
        & (block[None, :] // own_count == block[:, None] // own_count)
        & (block[None, :] < block[:, None]),
        axis=1,
    )
    table = ((block // own_count) ^ feat_index) * cap + before
    position = jnp.sum(
        jnp.where(mine[:, None] == block[None, :], table[None, :], 0), axis=1
    ).astype(jnp.int32)
    entry = jnp.arange(entries, dtype=jnp.int32)
    earlier = jnp.sum((mine[None, :] == mine[:, None]) & (entry[None, :] < entry[:, None]), axis=1)
    uses = entries // (feat_count * cap)
    key = position * uses + earlier
    order = jnp.sum(jnp.where(key[None, :] == entry[:, None], entry[None, :], 0), axis=1)
    return send, position, order.astype(jnp.int32)


def program(documents, expand_weight, sparse_weight, feature_lists, positives):
    feat_count = lax.axis_size("feat")
    label_count = lax.axis_size("label")
    feat_index = lax.axis_index("feat")
    label_index = lax.axis_index("label")
    group = feat_index * label_count + label_index
    ring = label_count // CORES
    ring_index, core = label_index // CORES, label_index % CORES
    docs = documents.shape[0]
    _, width = expand_weight.shape
    own_count = width // BLK
    own_blocks = own_count // label_count
    label_blocks, slots = sparse_weight.shape[:2]
    cap = CAP
    edges = [docs * sum(CHUNK_TENTHS[:i]) // 10 for i in range(len(CHUNK_TENTHS) + 1)]
    cuts = [slice(start, end) for start, end in zip(edges[:-1], edges[1:])]

    ring_width = width // ring
    starts = (jnp.arange(ring, dtype=jnp.int32) ^ ring_index) * ring_width

    def product(left, right):
        right = right.reshape(right.shape[0], ring_width // BLK, BLK)
        return jnp.einsum("dk,kbc->bdc", left, right, preferred_element_type=F32)

    columns = cut_columns(expand_weight, starts, ring_width)
    arrived = [columns[0]] + [None] * (ring - 1)
    for k in range(ring - 1, 0, -1):
        arrived[k] = ring_exchange(columns[k], k)
    documents_late, _ = lax.optimization_barrier((documents, columns[0]))
    expanded = product(documents, columns[0])
    for k in range(1, ring):
        other = ring_exchange(documents_late, k)
        expanded = expanded + product(other, arrived[k])
    kept = lax.dynamic_slice_in_dim(expanded, core * own_blocks, own_blocks, 0)
    given = lax.dynamic_slice_in_dim(expanded, (1 - core) * own_blocks, own_blocks, 0)

    block_weight = fetch(sparse_weight)
    send, position, order = list_tables(
        feature_lists, feat_index, label_index, label_count, own_count, label_blocks, cap
    )
    first_label = (group * label_blocks * BLK).reshape(1)
    known = [positives[cut] for cut in cuts]
    given, send, position, order, known, first_label = lax.optimization_barrier(
        (given, send, position, order, known, first_label)
    )
    hidden = jnp.maximum(kept + swap_cores(given), 0.0).astype(BF16)

    picked, residuals, gradients = [], [], []
    for i, cut in enumerate(cuts):
        pool = jnp.concatenate(ring_gather(hidden[:, cut]), axis=0)
        pools = [pool, swap_cores(pool)]
        outgoing = select_blocks(pools, send, cap)
        parts = [outgoing[0]] + [None] * (feat_count - 1)
        for m in range(feat_count - 1, 0, -1):
            parts[m] = feat_exchange(outgoing[m], m)
        residual, back = residual_and_back(
            parts, block_weight, position, order, known[i], first_label
        )
        picked.append(parts)
        residuals.append(residual)
        returned = [back[0]] + [None] * (feat_count - 1)
        for m in range(feat_count - 1, 0, -1):
            returned[m] = feat_exchange(back[m], m)
        kept, given = add_blocks(returned, send, own_count, CORES)
        both = (kept.astype(F32) + swap_cores(given).astype(F32)).astype(BF16)
        pieces = [both[k * own_blocks : (k + 1) * own_blocks] for k in range(ring)]
        total = pieces[0].astype(F32)
        for k in range(ring - 1, 0, -1):
            total = total + ring_exchange(pieces[k], k).astype(F32)
        if i:
            total, _ = lax.optimization_barrier((total, gradient))
        gradient = jnp.where(hidden[:, cut] > 0, total, 0.0).astype(BF16)
        gathered = jnp.concatenate(ring_gather(gradient), axis=0)
        gradients.append((gathered, swap_cores(gathered)))

    grad_sparse = None
    share = order.shape[0] // feat_count
    for m in range(feat_count):
        grad_sparse = block_weight_grad(
            grad_sparse,
            [parts[m] for parts in picked],
            residuals,
            order[m * share : (m + 1) * share],
            label_blocks,
            slots,
        )
    grad_sparse = grad_sparse.reshape(sparse_weight.shape)

    places = jnp.arange(CORES * ring, dtype=jnp.int32)
    owners = ((places % ring) ^ ring_index) * CORES + (places // ring ^ core)
    sides = [[gradient[side] for gradient in gradients] for side in range(CORES)]
    grad_expand = expand_weight_grad(
        documents, sides, owners * (own_blocks * BLK), own_blocks, width
    )
    return (grad_expand, grad_sparse)


def solution(mesh):
    return jax.shard_map(
        program,
        mesh=mesh,
        in_specs=(
            P(None, "label"),
            P("label", "feat"),
            P(("feat", "label"), None, None, None),
            P(),
            P(),
        ),
        out_specs=(P("label", "feat"), P(("feat", "label"), None, None, None)),
        check_vma=False,
    )
```

```python
import math

import jax
import jax.numpy as jnp
from jax import lax
from jax.experimental import pallas as pl
from jax.experimental.pallas import tpu as pltpu
from jax.sharding import PartitionSpec as P


BLK = 128
CAP = 24
CORES = 2
CHUNK_TENTHS = (3, 4, 3)
UNROLL = 4
SPARE_BYTES = 2 << 20
LATE_QUARTERS = 3

BF16 = jnp.bfloat16
F32 = jnp.float32
VMEM = pl.BlockSpec(memory_space=pltpu.VMEM)
SMEM = pl.BlockSpec(memory_space=pltpu.SMEM)
ANY = pl.BlockSpec(memory_space=pl.ANY)


def ring_exchange(x, flip):
    count = lax.axis_size("label")
    return lax.ppermute(x, "label", [(i, i ^ (flip * CORES)) for i in range(count)])


def swap_cores(x):
    count = lax.axis_size("label")
    return lax.ppermute(x, "label", [(i, i ^ 1) for i in range(count)])


def feat_exchange(x, flip):
    return lax.ppermute(x, "feat", [(i, i ^ flip) for i in range(lax.axis_size("feat"))])


def ring_gather(own):
    ring = lax.axis_size("label") // CORES
    return [own] + [ring_exchange(own, k) for k in range(1, ring)]


def grant(*blocks):
    total = 0
    for shape, dtype in blocks:
        total += math.prod(shape) * jnp.dtype(dtype).itemsize
    return pltpu.CompilerParams(vmem_limit_bytes=total + total // 8 + SPARE_BYTES)


def blocks_of(arrays):
    return [(x.shape, x.dtype) for x in arrays]


def cut_columns(weight, cuts):
    starts = jnp.stack([start for cut in cuts for start, _ in cut]).astype(jnp.int32)
    widths = [[width for _, width in cut] for cut in cuts]
    shapes = [(weight.shape[0], sum(width)) for width in widths]

    def kernel(starts_ref, weight_ref, *outs):
        at = 0
        for width, out in zip(widths, outs):
            done = 0
            for w in width:
                start = pl.multiple_of(starts_ref[at], BLK)
                out[:, done : done + w] = weight_ref[:, pl.ds(start, w)]
                done += w
                at += 1

    return pl.pallas_call(
        kernel,
        out_shape=[jax.ShapeDtypeStruct(shape, weight.dtype) for shape in shapes],
        in_specs=[SMEM, VMEM],
        out_specs=[VMEM] * len(cuts),
        compiler_params=grant((weight.shape, BF16), *[(shape, BF16) for shape in shapes]),
        name="cut_columns",
    )(starts, weight)


def expand_blocks(pairs, shorter, core):
    docs, _ = pairs[0][0].shape
    size = pairs[0][1].shape[1] // (CORES * BLK)
    every = pairs + shorter

    def kernel(core_ref, *refs):
        lefts, rights = refs[: len(every)], refs[len(every) : 2 * len(every)]
        for side, out in enumerate(refs[2 * len(every) :]):
            half = core_ref[0] if side == 0 else 1 - core_ref[0]
            total = None
            for left, right in zip(lefts, rights):
                width = right.shape[1] // CORES
                columns = right[:, pl.ds(pl.multiple_of(half * width, BLK), width)]
                term = jnp.dot(left[...], columns, preferred_element_type=F32)
                if total is None:
                    total = term
                elif width == size * BLK:
                    total = total + term
                else:
                    total = jnp.concatenate([total[:, :width] + term, total[:, width:]], axis=1)
            for j in range(size):
                out[j] = total[:, j * BLK : (j + 1) * BLK]

    shape = jax.ShapeDtypeStruct((size, docs, BLK), F32)
    lefts, rights = [left for left, _ in every], [right for _, right in every]
    return pl.pallas_call(
        kernel,
        out_shape=[shape] * CORES,
        in_specs=[SMEM] + [VMEM] * (2 * len(every)),
        out_specs=[VMEM] * CORES,
        compiler_params=grant(*blocks_of(lefts + rights), *[((4 * size, docs, BLK), F32)]),
        name="expand_blocks",
    )(core.reshape(1), *lefts, *rights)


def fetch(array):
    def kernel(source, target, sem):
        copy = pltpu.make_async_copy(source, target, sem)
        copy.start()
        copy.wait()

    return pl.pallas_call(
        kernel,
        out_shape=jax.ShapeDtypeStruct(array.shape, array.dtype),
        in_specs=[pl.BlockSpec(memory_space=pltpu.HBM)],
        out_specs=VMEM,
        scratch_shapes=[pltpu.SemaphoreType.DMA(())],
        compiler_params=grant((array.shape, array.dtype)),
        name="fetch",
    )(pltpu.with_memory_space_constraint(array, pltpu.HBM))


def select_blocks(pools, index, cap):
    size, docs, blk = pools[0].shape
    outs = index.shape[0] // cap

    def kernel(index_ref, *refs):
        ins = refs[: len(pools)]
        out_refs = refs[len(pools) :]
        for m in range(outs):

            def step(k, carry):
                place = index_ref[m * cap + k]
                block = ins[0][place % size]
                for i in range(1, len(ins)):
                    block = jnp.where(place >= i * size, ins[i][place % size], block)
                out_refs[m][k] = block
                return carry

            lax.fori_loop(0, cap, step, 0, unroll=UNROLL)

    return pl.pallas_call(
        kernel,
        out_shape=[jax.ShapeDtypeStruct((cap, docs, blk), BF16)] * outs,
        in_specs=[SMEM] + [VMEM] * len(pools),
        out_specs=[VMEM] * outs,
        compiler_params=grant(*blocks_of(pools), ((outs * cap, docs, blk), BF16)),
        name="select_blocks",
    )(index, *pools)


def add_blocks(parts, index, blocks, outs):
    cap, docs, blk = parts[0].shape
    size = blocks // outs

    def kernel(index_ref, *refs):
        ins = refs[: len(parts)]
        out_refs = refs[len(parts) : len(parts) + outs]
        total = refs[-1]
        total[...] = jnp.zeros_like(total)
        for m, ref in enumerate(ins):

            def step(k, carry):
                total[index_ref[m * cap + k]] += ref[k].astype(F32)
                return carry

            lax.fori_loop(0, cap, step, 0, unroll=UNROLL)
        for i, ref in enumerate(out_refs):
            ref[...] = total[pl.ds(i * size, size)].astype(BF16)

    return pl.pallas_call(
        kernel,
        out_shape=[jax.ShapeDtypeStruct((size, docs, blk), BF16)] * outs,
        in_specs=[SMEM] + [VMEM] * len(parts),
        out_specs=[VMEM] * outs,
        scratch_shapes=[pltpu.VMEM((blocks, docs, blk), F32)],
        compiler_params=grant(
            *blocks_of(parts), ((blocks, docs, blk), F32), ((blocks, docs, blk), BF16)
        ),
        name="add_blocks",
    )(index, *parts)


def residual_and_back(parts, weight, slot_position, order, positives, first_label):
    count = len(parts)
    cap, docs, blk = parts[0].shape
    label_blocks, slots = weight.shape[:2]
    uses = label_blocks * slots // (count * cap)
    pos_count = positives.shape[1]

    def kernel(position_ref, order_ref, first_ref, positives_ref, weight_ref, *refs):
        ins = refs[:count]
        residual_ref = refs[count]
        outs = refs[count + 1 : 2 * count + 1]
        pool, pool_sem = refs[2 * count + 1 :]
        copies = [
            pltpu.make_async_copy(ins[q], pool.at[pl.ds(q * cap, cap)], pool_sem.at[q])
            for q in range(count)
        ]
        for copy in copies:
            copy.start()
        for copy in copies:
            copy.wait()

        def forward(g, carry):
            lhs = jnp.concatenate(
                [pool[position_ref[g * slots + s]] for s in range(slots)], axis=1
            )
            rhs = weight_ref[g].reshape(slots * blk, blk)
            logits = jnp.dot(lhs, rhs, preferred_element_type=F32)
            ids = first_ref[0] + g * blk + lax.broadcasted_iota(jnp.int32, (docs, blk), 1)
            hit = positives_ref[:, 0:1] == ids
            for p in range(1, pos_count):
                hit = hit | (positives_ref[:, p : p + 1] == ids)
            residual_ref[g] = (jax.nn.sigmoid(logits) - jnp.where(hit, 1.0, 0.0)).astype(BF16)
            return carry

        lax.fori_loop(0, label_blocks, forward, 0, unroll=UNROLL)
        for q in range(count):

            def backward(k, carry):
                where = [order_ref[(q * cap + k) * uses + u] for u in range(uses)]
                lhs = jnp.concatenate([residual_ref[w // slots] for w in where], axis=1)
                rhs = jnp.concatenate([weight_ref[w // slots, w % slots] for w in where], axis=1)
                outs[q][k] = lax.dot_general(
                    lhs, rhs, (((1,), (1,)), ((), ())), preferred_element_type=F32
                ).astype(BF16)
                return carry

            lax.fori_loop(0, cap, backward, 0, unroll=2 * UNROLL)

    out = pl.pallas_call(
        kernel,
        out_shape=[jax.ShapeDtypeStruct((label_blocks, docs, blk), BF16)]
        + [jax.ShapeDtypeStruct((cap, docs, blk), BF16)] * count,
        in_specs=[SMEM] * 3 + [VMEM] * (2 + count),
        out_specs=[VMEM] * (count + 1),
        scratch_shapes=[
            pltpu.VMEM((count * cap, docs, blk), BF16),
            pltpu.SemaphoreType.DMA((count,)),
        ],
        compiler_params=grant(
            (weight.shape, BF16),
            ((3 * count * cap, docs, blk), BF16),
            ((label_blocks, docs, blk), BF16),
        ),
        name="residual_and_back",
    )(slot_position, order, first_label, positives, weight, *parts)
    return out[0], list(out[1:])


def block_weight_grad(so_far, picked, residuals, order, label_blocks, slots):
    pieces = len(picked)
    cap, _, blk = picked[0].shape
    uses = order.shape[0] // cap
    earlier = [] if so_far is None else [so_far]

    def kernel(order_ref, *refs):
        residual_refs = refs[:pieces]
        ins = refs[pieces : 2 * pieces]
        out_ref, buffer, sem = refs[2 * pieces + len(earlier) :]

        def step(k, carry):
            where = [order_ref[k * uses + u] for u in range(uses)]
            rhs = jnp.concatenate(
                [
                    jnp.concatenate([ref[w // slots] for w in where], axis=1)
                    for ref in residual_refs
                ],
                axis=0,
            )
            lhs = jnp.concatenate([ref[k] for ref in ins], axis=0)
            out = lax.dot_general(
                lhs, rhs, (((0,), (0,)), ((), ())), preferred_element_type=F32
            ).astype(BF16)
            for u in range(uses):
                buffer[k * uses + u] = out[:, u * blk : (u + 1) * blk]
                pltpu.make_async_copy(buffer.at[k * uses + u], out_ref.at[where[u]], sem).start()
            return carry

        lax.fori_loop(0, cap, step, 0, unroll=UNROLL)
        pltpu.make_async_copy(buffer, out_ref.at[pl.ds(0, cap * uses)], sem).wait()

    return pl.pallas_call(
        kernel,
        out_shape=jax.ShapeDtypeStruct((label_blocks * slots, blk, blk), BF16),
        in_specs=[SMEM] + [VMEM] * (2 * pieces) + [ANY] * len(earlier),
        out_specs=ANY,
        input_output_aliases={1 + 2 * pieces: 0} if earlier else {},
        scratch_shapes=[pltpu.VMEM((cap * uses, blk, blk), BF16), pltpu.SemaphoreType.DMA(())],
        compiler_params=grant(
            ((cap * uses, blk, blk), BF16), *blocks_of(picked), *blocks_of(residuals)
        ),
        name="block_weight_grad",
    )(order, *residuals, *picked, *earlier)


def expand_weight_grad(documents, sides, columns, size, width):
    chunks = len(sides[0])
    pieces = sides[0][0].shape[0] // size
    blk = sides[0][0].shape[2]
    _, rows = documents.shape

    def kernel(columns_ref, documents_ref, *refs):
        out_ref = refs[-1]
        lhs = documents_ref[...]
        for i in range(len(sides) * pieces):
            ins = refs[i // pieces * chunks : (i // pieces + 1) * chunks]
            blocks = range(i % pieces * size, (i % pieces + 1) * size)
            rhs = jnp.concatenate(
                [jnp.concatenate([ref[j] for ref in ins], axis=0) for j in blocks], axis=1
            )
            out = lax.dot_general(
                lhs, rhs, (((0,), (0,)), ((), ())), preferred_element_type=F32
            )
            start = pl.multiple_of(columns_ref[i], blk)
            out_ref[:, pl.ds(start, size * blk)] = out.astype(BF16)

    return pl.pallas_call(
        kernel,
        out_shape=jax.ShapeDtypeStruct((rows, width), BF16),
        in_specs=[SMEM, VMEM] + [VMEM] * (len(sides) * chunks),
        out_specs=VMEM,
        compiler_params=grant(
            ((rows, width), BF16), ((rows, width), F32), *blocks_of(sum(sides, []))
        ),
        name="expand_weight_grad",
    )(columns, documents, *[part for side in sides for part in side])


def list_tables(feature_lists, feat_index, label_index, label_count, own_count, label_blocks, cap):
    feat_count = lax.axis_size("feat")
    slots = feature_lists.shape[1]
    entries = label_blocks * slots
    ring = label_count // CORES
    own_blocks = own_count // label_count
    flips = jnp.arange(feat_count, dtype=jnp.int32)
    by_device = feature_lists.reshape(feat_count, label_count, entries)
    column = lax.dynamic_index_in_dim(by_device, label_index, 1, keepdims=False)
    mine = lax.dynamic_index_in_dim(column, feat_index, 0, keepdims=False)

    local = jnp.arange(own_count, dtype=jnp.int32)
    wanted = jnp.any(
        column[:, :, None] == (feat_index * own_count + local)[None, None, :], axis=1
    )
    rank = jnp.sum(wanted[:, None, :] & (local[None, :] < local[:, None])[None], axis=2)
    chosen = wanted[:, None, :] & (rank[:, None, :] == jnp.arange(cap)[None, :, None])
    ring_index, core = label_index // CORES, label_index % CORES
    owner_ring = local // (CORES * own_blocks)
    owner_core = local // own_blocks % CORES
    place = (
        jnp.where(owner_core == core, 0, ring) + (owner_ring ^ ring_index)
    ) * own_blocks + local % own_blocks
    send = jnp.sum(jnp.where(chosen, place[None, None, :], 0), axis=2).astype(jnp.int32)
    send = jnp.stack(
        [lax.dynamic_index_in_dim(send, feat_index ^ m, 0, keepdims=False) for m in range(feat_count)]
    ).reshape(-1)

    block = jnp.arange(feat_count * own_count, dtype=jnp.int32)
    present = jnp.any(mine[:, None] == block[None, :], axis=0)
    before = jnp.sum(
        present[None, :]
        & (block[None, :] // own_count == block[:, None] // own_count)
        & (block[None, :] < block[:, None]),
        axis=1,
    )
    table = ((block // own_count) ^ feat_index) * cap + before
    position = jnp.sum(
        jnp.where(mine[:, None] == block[None, :], table[None, :], 0), axis=1
    ).astype(jnp.int32)
    entry = jnp.arange(entries, dtype=jnp.int32)
    earlier = jnp.sum((mine[None, :] == mine[:, None]) & (entry[None, :] < entry[:, None]), axis=1)
    uses = entries // (feat_count * cap)
    key = position * uses + earlier
    order = jnp.sum(jnp.where(key[None, :] == entry[:, None], entry[None, :], 0), axis=1)
    return send, position, order.astype(jnp.int32)


def program(documents, expand_weight, sparse_weight, feature_lists, positives):
    feat_count = lax.axis_size("feat")
    label_count = lax.axis_size("label")
    feat_index = lax.axis_index("feat")
    label_index = lax.axis_index("label")
    group = feat_index * label_count + label_index
    ring = label_count // CORES
    ring_index, core = label_index // CORES, label_index % CORES
    docs = documents.shape[0]
    _, width = expand_weight.shape
    own_count = width // BLK
    own_blocks = own_count // label_count
    label_blocks, slots = sparse_weight.shape[:2]
    cap = CAP
    edges = [docs * sum(CHUNK_TENTHS[:i]) // 10 for i in range(len(CHUNK_TENTHS) + 1)]
    cuts = [slice(start, end) for start, end in zip(edges[:-1], edges[1:])]

    late_blocks = max(own_blocks * LATE_QUARTERS // 4, 1)
    raw_blocks = own_blocks - late_blocks
    pairs = range(2, ring, 2)

    def part(place, first, count):
        return [((place * CORES + c) * own_blocks * BLK + first * BLK, count * BLK) for c in range(CORES)]

    cut_list = [part(ring_index, 0, own_blocks), part(ring_index ^ 1, 0, own_blocks)]
    cut_list += [part(ring_index ^ k, 0, raw_blocks) for k in range(2, ring)]
    cut_list += [part(ring_index ^ k ^ 1, raw_blocks, late_blocks) for k in pairs]
    cut_list += [part(ring_index ^ k, raw_blocks, late_blocks) for k in pairs]
    pieces = cut_columns(expand_weight, cut_list)
    own, near, raw = pieces[0], pieces[1], [None] * 2 + list(pieces[2:ring])
    lent = dict(zip(pairs, pieces[ring:]))
    late = dict(zip(pairs, pieces[ring + len(pairs) :]))
    documents_late, _ = lax.optimization_barrier((documents, own))
    lent = {k: ring_exchange(lent[k], 1) for k in pairs}
    beside = ring_exchange(documents_late, 1)
    raw = raw[:2] + [ring_exchange(raw[k], k) for k in range(2, ring)]
    near = ring_exchange(near, 1)
    others = [None] * 2 + [ring_exchange(documents_late, k) for k in range(2, ring)]
    sums = {}
    for k in pairs:
        kept, given = expand_blocks([(documents, late[k]), (beside, lent[k])], [], core)
        sums[k] = kept + swap_cores(given)
    kept, given = expand_blocks(
        [(documents, own), (beside, near)],
        [(others[k], raw[k]) for k in range(2, ring)] if raw_blocks else [],
        core,
    )

    block_weight = fetch(sparse_weight)
    send, position, order = list_tables(
        feature_lists, feat_index, label_index, label_count, own_count, label_blocks, cap
    )
    first_label = (group * label_blocks * BLK).reshape(1)
    known = [positives[cut] for cut in cuts]
    given, send, position, order, known, first_label = lax.optimization_barrier(
        (given, send, position, order, known, first_label)
    )
    expanded = kept + swap_cores(given)

    picked, residuals, gradients = [], [], []
    for i, cut in enumerate(cuts):
        whole = expanded[:, cut]
        sent = [sums[k][:, cut] for k in pairs]
        if i:
            whole, sent, _ = lax.optimization_barrier((whole, sent, hidden))
        far = sum(ring_exchange(x, k) for x, k in zip(sent, pairs))
        whole = jnp.concatenate([whole[:raw_blocks], whole[raw_blocks:] + far], axis=0)
        hidden = jnp.maximum(whole, 0.0).astype(BF16)
        pool = jnp.concatenate(ring_gather(hidden), axis=0)
        pools = [pool, swap_cores(pool)]
        outgoing = select_blocks(pools, send, cap)
        parts = [outgoing[0]] + [None] * (feat_count - 1)
        for m in range(feat_count - 1, 0, -1):
            parts[m] = feat_exchange(outgoing[m], m)
        residual, back = residual_and_back(
            parts, block_weight, position, order, known[i], first_label
        )
        picked.append(parts)
        residuals.append(residual)
        returned = [back[0]] + [None] * (feat_count - 1)
        for m in range(feat_count - 1, 0, -1):
            returned[m] = feat_exchange(back[m], m)
        kept, given = add_blocks(returned, send, own_count, CORES)
        both = (kept.astype(F32) + swap_cores(given).astype(F32)).astype(BF16)
        pieces = [both[k * own_blocks : (k + 1) * own_blocks] for k in range(ring)]
        total = pieces[0].astype(F32)
        for k in range(ring - 1, 0, -1):
            total = total + ring_exchange(pieces[k], k).astype(F32)
        if i:
            total, _ = lax.optimization_barrier((total, gradient))
        gradient = jnp.where(hidden > 0, total, 0.0).astype(BF16)
        gathered = jnp.concatenate(ring_gather(gradient), axis=0)
        gradients.append((gathered, swap_cores(gathered)))

    grad_sparse = None
    share = order.shape[0] // feat_count
    for m in range(feat_count):
        grad_sparse = block_weight_grad(
            grad_sparse,
            [parts[m] for parts in picked],
            residuals,
            order[m * share : (m + 1) * share],
            label_blocks,
            slots,
        )
    grad_sparse = grad_sparse.reshape(sparse_weight.shape)

    places = jnp.arange(CORES * ring, dtype=jnp.int32)
    owners = ((places % ring) ^ ring_index) * CORES + (places // ring ^ core)
    sides = [[gradient[side] for gradient in gradients] for side in range(CORES)]
    grad_expand = expand_weight_grad(
        documents, sides, owners * (own_blocks * BLK), own_blocks, width
    )
    return (grad_expand, grad_sparse)


def solution(mesh):
    return jax.shard_map(
        program,
        mesh=mesh,
        in_specs=(
            P(None, "label"),
            P("label", "feat"),
            P(("feat", "label"), None, None, None),
            P(),
            P(),
        ),
        out_specs=(P("label", "feat"), P(("feat", "label"), None, None, None)),
        check_vma=False,
    )
```

```python
import math

import jax
import jax.numpy as jnp
from jax import lax
from jax.experimental import pallas as pl
from jax.experimental.pallas import tpu as pltpu
from jax.sharding import PartitionSpec as P


BLK = 128
CAP = 24
CORES = 2
CHUNK_TENTHS = (3, 4, 3)
UNROLL = 4
SPARE_BYTES = 2 << 20

BF16 = jnp.bfloat16
F32 = jnp.float32
VMEM = pl.BlockSpec(memory_space=pltpu.VMEM)
SMEM = pl.BlockSpec(memory_space=pltpu.SMEM)
ANY = pl.BlockSpec(memory_space=pl.ANY)


def ring_exchange(x, flip):
    count = lax.axis_size("label")
    return lax.ppermute(x, "label", [(i, i ^ (flip * CORES)) for i in range(count)])


def swap_cores(x):
    count = lax.axis_size("label")
    return lax.ppermute(x, "label", [(i, i ^ 1) for i in range(count)])


def feat_exchange(x, flip):
    return lax.ppermute(x, "feat", [(i, i ^ flip) for i in range(lax.axis_size("feat"))])


def ring_gather(own):
    ring = lax.axis_size("label") // CORES
    return [own] + [ring_exchange(own, k) for k in range(1, ring)]


def grant(*blocks):
    total = 0
    for shape, dtype in blocks:
        total += math.prod(shape) * jnp.dtype(dtype).itemsize
    return pltpu.CompilerParams(vmem_limit_bytes=total + total // 8 + SPARE_BYTES)


def blocks_of(arrays):
    return [(x.shape, x.dtype) for x in arrays]


def cut_columns(weight, starts, width):
    count = starts.shape[0]
    shape = (weight.shape[0], width)

    def kernel(starts_ref, weight_ref, *outs):
        for i, out in enumerate(outs):
            out[...] = weight_ref[:, pl.ds(pl.multiple_of(starts_ref[i], BLK), width)]

    return pl.pallas_call(
        kernel,
        out_shape=[jax.ShapeDtypeStruct(shape, weight.dtype)] * count,
        in_specs=[SMEM, VMEM],
        out_specs=[VMEM] * count,
        compiler_params=grant((weight.shape, BF16), ((count, *shape), BF16)),
        name="cut_columns",
    )(starts, weight)


def expand_blocks(pairs, core):
    docs = pairs[0][0].shape[0]
    half = pairs[0][1].shape[1] // CORES
    size = half // BLK

    def kernel(core_ref, *refs):
        lefts, rights = refs[: len(pairs)], refs[len(pairs) : 2 * len(pairs)]
        for side, out in enumerate(refs[2 * len(pairs) :]):
            which = core_ref[0] if side == 0 else 1 - core_ref[0]
            columns = pl.ds(pl.multiple_of(which * half, BLK), half)
            total = sum(
                jnp.dot(left[...], right[:, columns], preferred_element_type=F32)
                for left, right in zip(lefts, rights)
            )
            for j in range(size):
                out[j] = total[:, j * BLK : (j + 1) * BLK]

    lefts, rights = [left for left, _ in pairs], [right for _, right in pairs]
    return pl.pallas_call(
        kernel,
        out_shape=[jax.ShapeDtypeStruct((size, docs, BLK), F32)] * CORES,
        in_specs=[SMEM] + [VMEM] * (2 * len(pairs)),
        out_specs=[VMEM] * CORES,
        compiler_params=grant(*blocks_of(lefts + rights), ((4 * size, docs, BLK), F32)),
        name="expand_blocks",
    )(core.reshape(1), *lefts, *rights)


def fetch(array):
    def kernel(source, target, sem):
        copy = pltpu.make_async_copy(source, target, sem)
        copy.start()
        copy.wait()

    return pl.pallas_call(
        kernel,
        out_shape=jax.ShapeDtypeStruct(array.shape, array.dtype),
        in_specs=[pl.BlockSpec(memory_space=pltpu.HBM)],
        out_specs=VMEM,
        scratch_shapes=[pltpu.SemaphoreType.DMA(())],
        compiler_params=grant((array.shape, array.dtype)),
        name="fetch",
    )(pltpu.with_memory_space_constraint(array, pltpu.HBM))


def select_blocks(pools, index, cap):
    size, docs, blk = pools[0].shape
    outs = index.shape[0] // cap

    def kernel(index_ref, *refs):
        ins = refs[: len(pools)]
        out_refs = refs[len(pools) :]
        for m in range(outs):

            def step(k, carry):
                place = index_ref[m * cap + k]
                block = ins[0][place % size]
                for i in range(1, len(ins)):
                    block = jnp.where(place >= i * size, ins[i][place % size], block)
                out_refs[m][k] = block
                return carry

            lax.fori_loop(0, cap, step, 0, unroll=UNROLL)

    return pl.pallas_call(
        kernel,
        out_shape=[jax.ShapeDtypeStruct((cap, docs, blk), BF16)] * outs,
        in_specs=[SMEM] + [VMEM] * len(pools),
        out_specs=[VMEM] * outs,
        compiler_params=grant(*blocks_of(pools), ((outs * cap, docs, blk), BF16)),
        name="select_blocks",
    )(index, *pools)


def add_blocks(parts, index, blocks, outs):
    cap, docs, blk = parts[0].shape
    size = blocks // outs

    def kernel(index_ref, *refs):
        ins = refs[: len(parts)]
        out_refs = refs[len(parts) : len(parts) + outs]
        total = refs[-1]
        total[...] = jnp.zeros_like(total)
        for m, ref in enumerate(ins):

            def step(k, carry):
                total[index_ref[m * cap + k]] += ref[k].astype(F32)
                return carry

            lax.fori_loop(0, cap, step, 0, unroll=UNROLL)
        for i, ref in enumerate(out_refs):
            ref[...] = total[pl.ds(i * size, size)].astype(BF16)

    return pl.pallas_call(
        kernel,
        out_shape=[jax.ShapeDtypeStruct((size, docs, blk), BF16)] * outs,
        in_specs=[SMEM] + [VMEM] * len(parts),
        out_specs=[VMEM] * outs,
        scratch_shapes=[pltpu.VMEM((blocks, docs, blk), F32)],
        compiler_params=grant(
            *blocks_of(parts), ((blocks, docs, blk), F32), ((blocks, docs, blk), BF16)
        ),
        name="add_blocks",
    )(index, *parts)


def residual_and_back(parts, weight, slot_position, order, positives, first_label):
    count = len(parts)
    cap, docs, blk = parts[0].shape
    label_blocks, slots = weight.shape[:2]
    uses = label_blocks * slots // (count * cap)
    pos_count = positives.shape[1]

    def kernel(position_ref, order_ref, first_ref, positives_ref, weight_ref, *refs):
        ins = refs[:count]
        residual_ref = refs[count]
        outs = refs[count + 1 : 2 * count + 1]
        pool, pool_sem = refs[2 * count + 1 :]
        copies = [
            pltpu.make_async_copy(ins[q], pool.at[pl.ds(q * cap, cap)], pool_sem.at[q])
            for q in range(count)
        ]
        for copy in copies:
            copy.start()
        for copy in copies:
            copy.wait()

        def forward(g, carry):
            lhs = jnp.concatenate(
                [pool[position_ref[g * slots + s]] for s in range(slots)], axis=1
            )
            rhs = weight_ref[g].reshape(slots * blk, blk)
            logits = jnp.dot(lhs, rhs, preferred_element_type=F32)
            ids = first_ref[0] + g * blk + lax.broadcasted_iota(jnp.int32, (docs, blk), 1)
            hit = positives_ref[:, 0:1] == ids
            for p in range(1, pos_count):
                hit = hit | (positives_ref[:, p : p + 1] == ids)
            residual_ref[g] = (jax.nn.sigmoid(logits) - jnp.where(hit, 1.0, 0.0)).astype(BF16)
            return carry

        lax.fori_loop(0, label_blocks, forward, 0, unroll=UNROLL)
        for q in range(count):

            def backward(k, carry):
                where = [order_ref[(q * cap + k) * uses + u] for u in range(uses)]
                lhs = jnp.concatenate([residual_ref[w // slots] for w in where], axis=1)
                rhs = jnp.concatenate([weight_ref[w // slots, w % slots] for w in where], axis=1)
                outs[q][k] = lax.dot_general(
                    lhs, rhs, (((1,), (1,)), ((), ())), preferred_element_type=F32
                ).astype(BF16)
                return carry

            lax.fori_loop(0, cap, backward, 0, unroll=2 * UNROLL)

    out = pl.pallas_call(
        kernel,
        out_shape=[jax.ShapeDtypeStruct((label_blocks, docs, blk), BF16)]
        + [jax.ShapeDtypeStruct((cap, docs, blk), BF16)] * count,
        in_specs=[SMEM] * 3 + [VMEM] * (2 + count),
        out_specs=[VMEM] * (count + 1),
        scratch_shapes=[
            pltpu.VMEM((count * cap, docs, blk), BF16),
            pltpu.SemaphoreType.DMA((count,)),
        ],
        compiler_params=grant(
            (weight.shape, BF16),
            ((3 * count * cap, docs, blk), BF16),
            ((label_blocks, docs, blk), BF16),
        ),
        name="residual_and_back",
    )(slot_position, order, first_label, positives, weight, *parts)
    return out[0], list(out[1:])


def block_weight_grad(so_far, picked, residuals, order, label_blocks, slots):
    pieces = len(picked)
    cap, _, blk = picked[0].shape
    uses = order.shape[0] // cap
    earlier = [] if so_far is None else [so_far]

    def kernel(order_ref, *refs):
        residual_refs = refs[:pieces]
        ins = refs[pieces : 2 * pieces]
        out_ref, buffer, sem = refs[2 * pieces + len(earlier) :]

        def step(k, carry):
            where = [order_ref[k * uses + u] for u in range(uses)]
            rhs = jnp.concatenate(
                [
                    jnp.concatenate([ref[w // slots] for w in where], axis=1)
                    for ref in residual_refs
                ],
                axis=0,
            )
            lhs = jnp.concatenate([ref[k] for ref in ins], axis=0)
            out = lax.dot_general(
                lhs, rhs, (((0,), (0,)), ((), ())), preferred_element_type=F32
            ).astype(BF16)
            for u in range(uses):
                buffer[k * uses + u] = out[:, u * blk : (u + 1) * blk]
                pltpu.make_async_copy(buffer.at[k * uses + u], out_ref.at[where[u]], sem).start()
            return carry

        lax.fori_loop(0, cap, step, 0, unroll=UNROLL)
        pltpu.make_async_copy(buffer, out_ref.at[pl.ds(0, cap * uses)], sem).wait()

    return pl.pallas_call(
        kernel,
        out_shape=jax.ShapeDtypeStruct((label_blocks * slots, blk, blk), BF16),
        in_specs=[SMEM] + [VMEM] * (2 * pieces) + [ANY] * len(earlier),
        out_specs=ANY,
        input_output_aliases={1 + 2 * pieces: 0} if earlier else {},
        scratch_shapes=[pltpu.VMEM((cap * uses, blk, blk), BF16), pltpu.SemaphoreType.DMA(())],
        compiler_params=grant(
            ((cap * uses, blk, blk), BF16), *blocks_of(picked), *blocks_of(residuals)
        ),
        name="block_weight_grad",
    )(order, *residuals, *picked, *earlier)


def expand_weight_grad(documents, sides, columns, size, width):
    chunks = len(sides[0])
    pieces = sides[0][0].shape[0] // size
    blk = sides[0][0].shape[2]
    _, rows = documents.shape

    def kernel(columns_ref, documents_ref, *refs):
        out_ref = refs[-1]
        lhs = documents_ref[...]
        for i in range(len(sides) * pieces):
            ins = refs[i // pieces * chunks : (i // pieces + 1) * chunks]
            blocks = range(i % pieces * size, (i % pieces + 1) * size)
            rhs = jnp.concatenate(
                [jnp.concatenate([ref[j] for ref in ins], axis=0) for j in blocks], axis=1
            )
            out = lax.dot_general(
                lhs, rhs, (((0,), (0,)), ((), ())), preferred_element_type=F32
            )
            start = pl.multiple_of(columns_ref[i], blk)
            out_ref[:, pl.ds(start, size * blk)] = out.astype(BF16)

    return pl.pallas_call(
        kernel,
        out_shape=jax.ShapeDtypeStruct((rows, width), BF16),
        in_specs=[SMEM, VMEM] + [VMEM] * (len(sides) * chunks),
        out_specs=VMEM,
        compiler_params=grant(
            ((rows, width), BF16), ((rows, width), F32), *blocks_of(sum(sides, []))
        ),
        name="expand_weight_grad",
    )(columns, documents, *[part for side in sides for part in side])


def list_tables(feature_lists, feat_index, label_index, label_count, own_count, label_blocks, cap):
    feat_count = lax.axis_size("feat")
    slots = feature_lists.shape[1]
    entries = label_blocks * slots
    ring = label_count // CORES
    own_blocks = own_count // label_count
    flips = jnp.arange(feat_count, dtype=jnp.int32)
    by_device = feature_lists.reshape(feat_count, label_count, entries)
    column = lax.dynamic_index_in_dim(by_device, label_index, 1, keepdims=False)
    mine = lax.dynamic_index_in_dim(column, feat_index, 0, keepdims=False)

    local = jnp.arange(own_count, dtype=jnp.int32)
    wanted = jnp.any(
        column[:, :, None] == (feat_index * own_count + local)[None, None, :], axis=1
    )
    rank = jnp.sum(wanted[:, None, :] & (local[None, :] < local[:, None])[None], axis=2)
    chosen = wanted[:, None, :] & (rank[:, None, :] == jnp.arange(cap)[None, :, None])
    ring_index, core = label_index // CORES, label_index % CORES
    owner_ring = local // (CORES * own_blocks)
    owner_core = local // own_blocks % CORES
    place = (
        jnp.where(owner_core == core, 0, ring) + (owner_ring ^ ring_index)
    ) * own_blocks + local % own_blocks
    send = jnp.sum(jnp.where(chosen, place[None, None, :], 0), axis=2).astype(jnp.int32)
    send = jnp.stack(
        [lax.dynamic_index_in_dim(send, feat_index ^ m, 0, keepdims=False) for m in range(feat_count)]
    ).reshape(-1)

    block = jnp.arange(feat_count * own_count, dtype=jnp.int32)
    present = jnp.any(mine[:, None] == block[None, :], axis=0)
    before = jnp.sum(
        present[None, :]
        & (block[None, :] // own_count == block[:, None] // own_count)
        & (block[None, :] < block[:, None]),
        axis=1,
    )
    table = ((block // own_count) ^ feat_index) * cap + before
    position = jnp.sum(
        jnp.where(mine[:, None] == block[None, :], table[None, :], 0), axis=1
    ).astype(jnp.int32)
    entry = jnp.arange(entries, dtype=jnp.int32)
    earlier = jnp.sum((mine[None, :] == mine[:, None]) & (entry[None, :] < entry[:, None]), axis=1)
    uses = entries // (feat_count * cap)
    key = position * uses + earlier
    order = jnp.sum(jnp.where(key[None, :] == entry[:, None], entry[None, :], 0), axis=1)
    return send, position, order.astype(jnp.int32)


def program(documents, expand_weight, sparse_weight, feature_lists, positives):
    feat_count = lax.axis_size("feat")
    label_count = lax.axis_size("label")
    feat_index = lax.axis_index("feat")
    label_index = lax.axis_index("label")
    group = feat_index * label_count + label_index
    ring = label_count // CORES
    ring_index, core = label_index // CORES, label_index % CORES
    docs = documents.shape[0]
    _, width = expand_weight.shape
    own_count = width // BLK
    own_blocks = own_count // label_count
    label_blocks, slots = sparse_weight.shape[:2]
    cap = CAP
    edges = [docs * sum(CHUNK_TENTHS[:i]) // 10 for i in range(len(CHUNK_TENTHS) + 1)]
    cuts = [slice(start, end) for start, end in zip(edges[:-1], edges[1:])]

    pairs = range(2, ring, 2)
    ring_width = width // ring

    places = [ring_index, ring_index ^ 1]
    places += [ring_index ^ k ^ 1 for k in pairs] + [ring_index ^ k for k in pairs]
    pieces = cut_columns(expand_weight, jnp.stack(places) * ring_width, ring_width)
    own, near = pieces[:2]
    lent = dict(zip(pairs, pieces[2:]))
    late = dict(zip(pairs, pieces[2 + len(pairs) :]))
    documents_late, _ = lax.optimization_barrier((documents, own))
    lent = {k: ring_exchange(lent[k], 1) for k in pairs}
    beside = ring_exchange(documents_late, 1)
    near = ring_exchange(near, 1)
    sums = {}
    for k in pairs:
        kept, given = expand_blocks([(documents, late[k]), (beside, lent[k])], core)
        sums[k] = kept + swap_cores(given)
    kept, given = expand_blocks([(documents, own), (beside, near)], core)

    block_weight = fetch(sparse_weight)
    send, position, order = list_tables(
        feature_lists, feat_index, label_index, label_count, own_count, label_blocks, cap
    )
    first_label = (group * label_blocks * BLK).reshape(1)
    known = [positives[cut] for cut in cuts]
    given, send, position, order, known, first_label = lax.optimization_barrier(
        (given, send, position, order, known, first_label)
    )
    expanded = kept + swap_cores(given)

    picked, residuals, gradients = [], [], []
    for i, cut in enumerate(cuts):
        whole = expanded[:, cut]
        far = sum(ring_exchange(sums[k][:, cut], k) for k in pairs)
        if i:
            whole, far, _ = lax.optimization_barrier((whole, far, hidden))
        hidden = jnp.maximum(whole + far, 0.0).astype(BF16)
        pool = jnp.concatenate(ring_gather(hidden), axis=0)
        pools = [pool, swap_cores(pool)]
        outgoing = select_blocks(pools, send, cap)
        parts = [outgoing[0]] + [None] * (feat_count - 1)
        for m in range(feat_count - 1, 0, -1):
            parts[m] = feat_exchange(outgoing[m], m)
        residual, back = residual_and_back(
            parts, block_weight, position, order, known[i], first_label
        )
        picked.append(parts)
        residuals.append(residual)
        returned = [back[0]] + [None] * (feat_count - 1)
        for m in range(feat_count - 1, 0, -1):
            returned[m] = feat_exchange(back[m], m)
        kept, given = add_blocks(returned, send, own_count, CORES)
        both = (kept.astype(F32) + swap_cores(given).astype(F32)).astype(BF16)
        pieces = [both[k * own_blocks : (k + 1) * own_blocks] for k in range(ring)]
        total = pieces[0].astype(F32)
        for k in range(ring - 1, 0, -1):
            total = total + ring_exchange(pieces[k], k).astype(F32)
        if i:
            total, _ = lax.optimization_barrier((total, gradient))
        gradient = jnp.where(hidden > 0, total, 0.0).astype(BF16)
        gathered = jnp.concatenate(ring_gather(gradient), axis=0)
        gradients.append((gathered, swap_cores(gathered)))

    grad_sparse = None
    share = order.shape[0] // feat_count
    for m in range(feat_count):
        grad_sparse = block_weight_grad(
            grad_sparse,
            [parts[m] for parts in picked],
            residuals,
            order[m * share : (m + 1) * share],
            label_blocks,
            slots,
        )
    grad_sparse = grad_sparse.reshape(sparse_weight.shape)

    places = jnp.arange(CORES * ring, dtype=jnp.int32)
    owners = ((places % ring) ^ ring_index) * CORES + (places // ring ^ core)
    sides = [[gradient[side] for gradient in gradients] for side in range(CORES)]
    grad_expand = expand_weight_grad(
        documents, sides, owners * (own_blocks * BLK), own_blocks, width
    )
    return (grad_expand, grad_sparse)


def solution(mesh):
    return jax.shard_map(
        program,
        mesh=mesh,
        in_specs=(
            P(None, "label"),
            P("label", "feat"),
            P(("feat", "label"), None, None, None),
            P(),
            P(),
        ),
        out_specs=(P("label", "feat"), P(("feat", "label"), None, None, None)),
        check_vma=False,
    )
```
